128 devices in a mesh: net: 8 (over x, core), rep: 16 (over y, z).
Axes of the slice: x: 4, y: 4, z: 4, core: 2. Of those that a mesh axis runs over, the one named last changes fastest.
Arguments:
- latent: bfloat16 [64, 64, 256], P('net', 'rep'), may hold values from -7.2 to 7.2
- hint: bfloat16 [64, 64, 64, 192], P('net', 'rep'), may hold values from -6 to 6
- cond_ids: int32 [64, 1], P('net'), may hold values from 0 to 7; in each aligned block of 8 rows (0 to 7, 8 to 15, ...) at most 2 rows name the same one
- valid: int32 [64], P('net'), may hold values 0 or 1
- cond_scale: float32 [64], P('net'), may hold values from 0.5 to 1.5
- ctl_in: bfloat16 [8, 3, 3, 4, 320], P('net'), may hold values from -1 to 1
- ctl_hint: bfloat16 [8, 192, 320], P('net'), may hold values from -0.4375 to 0.4375
- ctl_zero0: bfloat16 [8, 320, 320], P('net'), may hold values from -0.3125 to 0.3125
- ctl_gain: bfloat16 [8, 320], P('net'), may hold values from 0.099609375 to 1.8984375
- ctl_conv: bfloat16 [8, 3, 3, 320, 320], P('net'), may hold values from -0.109375 to 0.109375
- ctl_zero1: bfloat16 [8, 320, 320], P('net'), may hold values from -0.3125 to 0.3125
- unet_in: bfloat16 [3, 3, 4, 320], replicated, may hold values from -1 to 1
- unet_gain: bfloat16 [320], replicated, may hold values from 0.099609375 to 1.8984375
- unet_conv: bfloat16 [3, 3, 320, 320], replicated, may hold values from -0.109375 to 0.109375
Outputs:
- skip0: bfloat16 [64, 64, 64, 320], P('net', 'rep')
- skip1: bfloat16 [64, 64, 64, 320], P('net', 'rep')
The draws below stay inside these ranges and needn't reach their ends.
Inputs may be any that keep to these rules, and one draw needn't show every extreme that they name: `cond_ids`: in each aligned block of 8 requests (those of one index of net) no id is named by more than 2 requests.
All inputs are finite; a program needn't handle non-finite values. No bound on the sum of `valid` on one device may be relied on, other than what follows from the above.
Results may differ from the reference program's by a relative error of at most 0.008.
Values may be sent and summed in bfloat16 or wider, within the bound.
A program may use at most 256 MiB of HBM per device.

```python
import math
import jax
import jax.numpy as jnp
import numpy as np
from jax import lax

CH = 320
LCH = 4
GROUPS = 32
HINT = 192
LAT = 64
REQ_GROUP = 8
NETS = 8
PAIR_CAP = 2
REQUESTS = 64
N_NET = 8


def draw_latent(key, part):
    row_place = jnp.arange(LAT, dtype=jnp.float32) / (LAT - 1)
    row_scale = jnp.exp(jnp.log(0.6) + row_place * jnp.log(3.0))
    values = jnp.clip(jax.random.normal(key, (REQUESTS, LAT, LAT * LCH), jnp.float32), -4.0, 4.0)
    return (values * row_scale[None, :, None]).astype(jnp.bfloat16)


def with_ends(entries, stream_key, smallest, top_value):
    longest = entries.shape.index(max(entries.shape))
    spots = []
    for shift in (0, 1):
        where = [jax.random.randint(jax.random.fold_in(stream_key, axis), (), 0, length) for axis, length in enumerate(entries.shape)]
        where[longest] = (where[longest] + shift) % entries.shape[longest]
        spots.append(tuple(where))
    return entries.at[spots[0]].set(smallest).at[spots[1]].set(top_value)


def block_levels(stream_key, shape, pieces, low, high):
    level = 1.0
    for axis_at, parts in pieces:
        heights = jax.random.uniform(jax.random.fold_in(jax.random.fold_in(stream_key, 6), axis_at), (parts,), jnp.float32, low / len(pieces), high / len(pieces))
        level = level * jnp.repeat(jnp.exp(heights), shape[axis_at] // parts).reshape((-1,) + (1,) * (len(shape) - 1 - axis_at))
    return level


def shared_out(rng, own, number, rows, number_of, top, limit, skew):
    order = jax.random.permutation(rng, number_of)
    packed, common = portions_of(number_of, rows * top, limit, skew, True), portions_of(number_of, rows * top, limit, skew, False)
    places = jnp.arange(number_of)

    def named(lengths, rotation):
        used = int((lengths > 0).sum())
        fixed = max(1, used // 4)
        shifted = fixed + (places - fixed + rotation * (used - fixed)) % max(1, number_of - fixed)
        return jnp.zeros((number_of,), jnp.int32).at[order[jnp.where(places < fixed, places, shifted)]].set(jnp.asarray(lengths, jnp.int32))

    lengths = jnp.where(number % 4 == 0, named(packed, number // 4), named(common, number - number // 4 - 1))
    mixed = jax.random.permutation(jax.random.fold_in(own, 3), number_of)
    donor, receiver = mixed[0:number_of // 2 * 2:2], mixed[1:number_of // 2 * 2:2]
    margin = jnp.minimum(lengths[donor] - 1, limit - lengths[receiver]) // 2
    margin = jnp.where((donor == order[0]) | (receiver == order[0]) | (lengths[receiver] == 0), 0, jnp.maximum(margin, 0))
    shifted = jax.random.randint(jax.random.fold_in(own, 4), (number_of // 2,), 0, 1 << 20) % (margin + 1)
    lengths = lengths.at[donor].add(-shifted).at[receiver].add(shifted)
    labels = jnp.searchsorted(jnp.cumsum(lengths), jnp.arange(rows * top), side="right").astype(jnp.int32)
    grid = labels.reshape(top, rows).T
    grid = grid[jax.random.permutation(jax.random.fold_in(own, 1), rows)]
    rotation = jax.random.randint(jax.random.fold_in(own, 2), (rows, 1), 0, top)
    return jnp.take_along_axis(grid, (jnp.arange(top)[None, :] + rotation) % top, axis=1)


def portions_of(amount, total, bound, lean, full):
    weights = [(1 << 20) // math.isqrt(standing ** lean) + 1 for standing in range(1, amount + 1)]
    largest = bound if full else min(bound, max(-(-total // amount), total * weights[0] // sum(weights)))
    least = 1 if total - largest >= amount - 1 else 0
    counts, rest = [largest] + [least] * (amount - 1), total - largest - least * (amount - 1)
    while rest > 0:
        free = [i for i in range(1, amount) if counts[i] < largest] or [i for i in range(1, amount) if counts[i] < bound]
        pool, remaining = sum([weights[i] for i in free]), rest
        for i in free:
            more = min(bound - counts[i], max(1, remaining * weights[i] // pool), rest)
            counts[i] = counts[i] + more
            rest = rest - more
    return np.array(counts)


def gaussian(own_key, dims, scale, most, pieces=(), held_as=jnp.bfloat16):
    values = jax.random.normal(own_key, dims, jnp.float32) * scale
    if len(pieces) > 0:
        values = block_levels(own_key, dims, pieces, -0.22, 0.18) * values
    return jnp.clip(values, min=-most, max=most).astype(held_as)


def setup_inputs(seed: int = 0) -> dict:
    key_list = jax.random.split(jax.random.key(seed), 15)
    latent = draw_latent(jax.random.fold_in(key_list[14], 71), 0)
    hint = gaussian(key_list[1], (REQUESTS, LAT, LAT, HINT), 1.0, 6.0, ((0, 8), (1, 16)))
    cond_ids_keys = jax.random.split(jax.random.fold_in(key_list[2], 1), REQUESTS // REQ_GROUP)
    cond_ids_turns = jax.random.permutation(jax.random.fold_in(key_list[2], 3), REQUESTS // REQ_GROUP)
    cond_ids = jax.vmap(lambda own, number: shared_out(jax.random.fold_in(key_list[2], 2), own, number, REQ_GROUP, N_NET, 1, PAIR_CAP, 2))(cond_ids_keys, cond_ids_turns).reshape((REQUESTS, 1))
    valid = with_ends((jax.random.randint(key_list[3], (REQUESTS,), 0, 8) < 7).astype(jnp.int32), jax.random.fold_in(key_list[3], 1), 0, 1)
    cond_scale = jnp.clip(0.5 + 1.0 * jax.random.uniform(key_list[4], (REQUESTS,), jnp.float32) ** block_levels(key_list[4], (REQUESTS,), ((0, 8),), -0.2, 0.2), 0.5, 1.5)
    ctl_in = gaussian(key_list[5], (NETS, 3, 3, LCH, CH), (9 * LCH) ** -0.5, 1.0, ((0, 8),))
    ctl_hint = gaussian(key_list[6], (NETS, HINT, CH), HINT ** -0.5, 0.4375, ((0, 8),))
    ctl_zero0 = gaussian(key_list[7], (NETS, CH, CH), CH ** -0.5, 0.3125, ((0, 8),))
    ctl_gain = jnp.clip(1.0 + 0.18 * jax.random.normal(key_list[8], (NETS, CH), jnp.float32), 0.099609375, 1.8984375).astype(jnp.bfloat16)
    ctl_conv = gaussian(key_list[9], (NETS, 3, 3, CH, CH), (9 * CH) ** -0.5, 0.109375, ((0, 8),))
    ctl_zero1 = gaussian(key_list[10], (NETS, CH, CH), CH ** -0.5, 0.3125, ((0, 8),))
    unet_in = gaussian(key_list[11], (3, 3, LCH, CH), (9 * LCH) ** -0.5, 1.0)
    unet_gain = jnp.clip(1.0 + 0.18 * jax.random.normal(key_list[12], (CH,), jnp.float32), 0.099609375, 1.8984375).astype(jnp.bfloat16)
    unet_conv = gaussian(key_list[13], (3, 3, CH, CH), (9 * CH) ** -0.5, 0.109375)
    return dict(latent=latent, hint=hint, cond_ids=cond_ids, valid=valid, cond_scale=cond_scale, ctl_in=ctl_in, ctl_hint=ctl_hint, ctl_zero0=ctl_zero0, ctl_gain=ctl_gain, ctl_conv=ctl_conv, ctl_zero1=ctl_zero1, unet_in=unet_in, unet_gain=unet_gain, unet_conv=unet_conv)


epsilon = 1e-05

def conv_rows(padded, weight):
    row_count = padded.shape[-3] - 2
    col_count = padded.shape[-2]
    padding = [(0, 0)] * (padded.ndim - 2) + [(1, 1), (0, 0)]
    padded_cols = jnp.pad(padded, padding)
    result = None
    for shift_y in range(3):
        for shift_x in range(3):
            window = padded_cols[..., shift_y:shift_y + row_count, shift_x:shift_x + col_count, :]
            contribution = jnp.dot(window.reshape(-1, window.shape[-1]), weight[shift_y, shift_x], preferred_element_type=jnp.float32)
            contribution = contribution.reshape(window.shape[:-1] + (weight.shape[-1],))
            result = contribution if result is None else result + contribution
    return result

def project(values, weight):
    flat_out = jnp.dot(values.reshape(-1, values.shape[-1]), weight, preferred_element_type=jnp.float32)
    return flat_out.reshape(values.shape[:-1] + (weight.shape[-1],))

def norm_silu(values, gain):
    floats = values.astype(jnp.float32)
    first_sums = lax.optimization_barrier(jnp.sum(floats, axis=(-3, -2)))
    second_sums = lax.optimization_barrier(jnp.sum(floats * floats, axis=(-3, -2)))
    group_size = values.shape[-1] // GROUPS
    count = values.shape[-3] * values.shape[-2] * group_size
    group_mean = first_sums.reshape(first_sums.shape[:-1] + (GROUPS, group_size)).sum(-1) / count
    group_square = second_sums.reshape(second_sums.shape[:-1] + (GROUPS, group_size)).sum(-1) / count
    inverse = lax.rsqrt(group_square - group_mean * group_mean + epsilon)
    mean_chan = jnp.repeat(group_mean, group_size, axis=-1)
    scale_chan = jnp.repeat(inverse, group_size, axis=-1) * gain.astype(jnp.float32)
    normed = (floats - mean_chan[..., None, None, :]) * scale_chan[..., None, None, :]
    return jax.nn.silu(normed).astype(jnp.bfloat16)

def pad_rows(values):
    return jnp.pad(values, ((1, 1), (0, 0), (0, 0)))

def reference(latent, hint, cond_ids, valid, cond_scale, ctl_in, ctl_hint, ctl_zero0, ctl_gain, ctl_conv, ctl_zero1, unet_in, unet_gain, unet_conv):

    def one_request(request):
        lat_flat, hint_grid, condition, scaling, live = request
        lat_grid = lat_flat.reshape(LAT, LAT, LCH)
        lat_padded = pad_rows(lat_grid)
        first_ctl = (conv_rows(lat_padded, ctl_in[condition]) + project(hint_grid, ctl_hint[condition])).astype(jnp.bfloat16)
        first_res = project(first_ctl, ctl_zero0[condition]).astype(jnp.bfloat16)
        ctl_normed = norm_silu(first_ctl, ctl_gain[condition])
        second_ctl = (first_ctl.astype(jnp.float32) + conv_rows(pad_rows(ctl_normed), ctl_conv[condition])).astype(jnp.bfloat16)
        second_res = project(second_ctl, ctl_zero1[condition]).astype(jnp.bfloat16)
        unet_first = conv_rows(lat_padded, unet_in).astype(jnp.bfloat16)
        unet_normed = norm_silu(unet_first, unet_gain)
        weighting = scaling * live.astype(jnp.float32)
        first_skip = (unet_first.astype(jnp.float32) + weighting * first_res.astype(jnp.float32)).astype(jnp.bfloat16)
        second_skip = (unet_first.astype(jnp.float32) + conv_rows(pad_rows(unet_normed), unet_conv) + weighting * second_res.astype(jnp.float32)).astype(jnp.bfloat16)
        return (first_skip, second_skip)
    skip_first, skip_second = lax.map(one_request, (latent, hint, cond_ids[:, 0], cond_scale, valid))
    return (skip_first, skip_second)
```

```python
import functools

import jax
import jax.numpy as jnp
from jax import lax
from jax.experimental import pallas as pl
from jax.experimental.pallas import tpu as pltpu
from jax.sharding import PartitionSpec as P

MESH = pl.DeviceIdType.MESH
F32, BF16 = jnp.float32, jnp.bfloat16
CH = 320
GROUPS = 32
REQ = 8
EPS = 1e-5
O_M, O_K, O_N, O_Z1, O_Z0, O_ZT, ROWS = 0, 2304, 2880, 3648, 3968, 4288, 4416
CHUNK = 256
E2 = 16 * CHUNK
E2N = ROWS - E2
E2H = E2N // 2
WHR = 256


def gray(v):
    return v + lax.div(v, 2) - 2 * lax.div(v, 3)


def gather_kernel(
    ids, latf, hint, wh, wu, blob, ugain, uconv,
    g, t_out, u_out, h_out, nm_out, nt_out,
    blobv, whs, hintb, latb, lat48, ub, hb, mb, tb, nmb, ntb, ucv, stu, sth,
    s_x, s_yz, s_e, s_wh, s_sib, s_whsib, s_send, s_whsend,
    s_halo, s_hsend, s_st, s_stsend, s_loc, s_out,
):
    net, rep = lax.axis_index("net"), lax.axis_index("rep")
    x, c = lax.div(net, 2), lax.rem(net, 2)
    y, z = lax.div(rep, 4), lax.rem(rep, 4)

    def dev(dx=0, dy=0, dz=0, dc=0):
        return (
            lax.rem(x + dx, 4) * 2 + lax.rem(c + dc, 2),
            lax.rem(y + dy, 4) * 4 + lax.rem(z + dz, 4),
        )

    def rdev(d):
        return (net, lax.rem(rep + d, 16))

    def colour(q, dy=0, dz=0):
        yy, zz = lax.rem(y + dy, 4), lax.rem(z + dz, 4)
        a, b = (yy, zz) if q == 0 else (zz, yy)
        ga, odd = gray(a), lax.rem(b, 2)
        return ga + odd * (3 - 2 * ga)

    def net_of(dx):
        return lax.rem(x + dx, 4) * 2 + c

    loads = [
        pltpu.make_async_copy(blob, blobv, s_loc.at[0]),
        pltpu.make_async_copy(hint, hintb.at[:, pl.ds(1, 4)], s_loc.at[1]),
        pltpu.make_async_copy(uconv, ucv, s_loc.at[2]),
    ]
    for cp in loads:
        cp.start()

    barrier = pltpu.get_barrier_semaphore()
    partners = [
        dev(dx=1), dev(dx=3), dev(dc=1), dev(dy=1), dev(dy=3), dev(dy=2),
        dev(dz=1), dev(dz=3), dev(dz=2), rdev(1), rdev(15),
    ]
    for p in partners:
        pl.semaphore_signal(barrier, inc=1, device_id=p, device_id_type=MESH)
    pl.semaphore_wait(barrier, len(partners))

    def send(src, dst, sem, where, ssem):
        pltpu.make_async_remote_copy(
            src_ref=src, dst_ref=dst, send_sem=ssem, recv_sem=sem,
            device_id=where, device_id_type=MESH,
        ).start()

    def arrived(ref, sem):
        pltpu.make_async_copy(ref, ref, sem).wait()

    EV = {}
    for q in range(2):
        for h in range(2):
            EV["L", q, h] = (3, q, h, q * 2 + h)
            EV["R", q, h] = (1, q, h, 4 + q * 2 + h)
        EV["LL", q] = (2, q, 0, 8 + q)
        EV["RR", q] = (2, q, 1, 10 + q)

    def rows_of(q, h, dy=0, dz=0):
        start = pl.multiple_of((colour(q, dy, dz) * 2 + (q * 8 + h)) * CHUNK, CHUNK)
        return pl.ds(start, CHUNK)

    def own_chunk(q, h):
        r = rows_of(q, h)
        send(blob.at[r], g.at[net, r], s_x.at[EV["L", q, h][3]], dev(dx=1), s_send)
        send(blob.at[r], g.at[net, r], s_x.at[EV["R", q, h][3]], dev(dx=3), s_send)

    def x_relay(key):
        dx, q, h, _ = EV[key]
        ref = g.at[net_of(dx), rows_of(q, h)]
        if key[0] == "L":
            send(ref, ref, s_x.at[EV["LL", q][3]], dev(dx=1), s_send)
        else:
            send(ref, ref, s_x.at[EV["RR", q][3]], dev(dx=3), s_send)

    def to_sib(ref):
        send(ref, ref, s_sib, dev(dc=1), s_send)

    def dirs(q, h):
        main, other = ((0, 1), (2, 3)) if q == 0 else ((2, 3), (0, 1))
        return main + (other[h],)

    STEP = [dict(dy=1), dict(dy=3), dict(dz=1), dict(dz=3)]
    BACK = [dict(dy=3), dict(dy=1), dict(dz=3), dict(dz=1)]

    def x_event(key):
        dx, q, h, sem = EV[key]
        ref = g.at[net_of(dx), rows_of(q, h)]
        arrived(ref, s_x.at[sem])
        for d in dirs(q, h):
            send(ref, ref, s_yz.at[d * 12 + sem], dev(**STEP[d]), s_send)
        to_sib(ref)

    def yz_event(key):
        dx, q, h, sem = EV[key]
        for d in dirs(q, h):
            ref = g.at[net_of(dx), rows_of(q, h, **BACK[d])]
            arrived(ref, s_yz.at[d * 12 + sem])
            to_sib(ref)

    e2r, e2h = pl.ds(E2, E2N), (pl.ds(E2, E2H), pl.ds(E2 + E2H, E2H))

    def own_e2():
        send(blob.at[e2r], g.at[net, e2r], s_e.at[0], dev(dx=1), s_send)
        send(blob.at[e2r], g.at[net, e2r], s_e.at[1], dev(dx=3), s_send)

    def e2_event():
        for i, dx, to in ((0, 3, 1), (1, 1, 3)):
            ref = g.at[net_of(dx), e2r]
            arrived(ref, s_e.at[i])
            half = g.at[net_of(dx), e2h[i]]
            send(half, half, s_e.at[2 + i], dev(dx=to), s_send)
            to_sib(ref)

    def e2_far():
        for i in range(2):
            ref = g.at[net_of(2), e2h[i]]
            arrived(ref, s_e.at[2 + i])
            to_sib(ref)

    whh = (pl.ds(0, WHR // 2), pl.ds(WHR // 2, WHR // 2))

    def wh_sib(ref):
        send(ref, ref, s_whsib, dev(dc=1), s_whsend)

    def wh_event():
        for i, dx, to in ((0, 3, 1), (1, 1, 3)):
            ref = whs.at[net_of(dx)]
            arrived(ref, s_wh.at[i])
            half = whs.at[net_of(dx), whh[i]]
            send(half, half, s_wh.at[2 + i], dev(dx=to), s_whsend)
            wh_sib(ref)

    def wh_far():
        for i in range(2):
            ref = whs.at[net_of(2), whh[i]]
            arrived(ref, s_wh.at[2 + i])
            wh_sib(ref)
        arrived(whs.at[pl.ds(0, 4)], s_whsib)

    halos = [
        (latf, latb.at[0], rdev(1)), (latf, latb.at[1], rdev(15)),
        (hint.at[:, 3], hintb.at[:, 0], rdev(1)), (hint.at[:, 0], hintb.at[:, 5], rdev(15)),
    ]
    for i, (src, dst, to) in enumerate(halos[:2]):
        send(src, dst, s_halo.at[i], to, s_hsend.at[i])
    own_chunk(0, 0)
    own_chunk(1, 0)
    send(wh, whs.at[net], s_wh.at[0], dev(dx=1), s_whsend)
    send(wh, whs.at[net], s_wh.at[1], dev(dx=3), s_whsend)
    send(wh, whs.at[net], s_whsib, dev(dc=1), s_whsend)
    send(blob, g.at[net], s_sib, dev(dc=1), s_send)
    for i, (src, dst, to) in enumerate(halos):
        if i >= 2:
            send(src, dst, s_halo.at[i], to, s_hsend.at[i])
    own_wh = pltpu.make_async_copy(wh, whs.at[net], s_loc.at[3])
    own_wh.start()
    loads[0].wait()
    own_blob = pltpu.make_async_copy(blobv, g.at[net], s_loc.at[4])
    own_blob.start()

    for i in range(2):
        arrived(latb.at[i], s_halo.at[i])
    li = lax.broadcasted_iota(jnp.int32, (256, 256), 0)
    lj = lax.broadcasted_iota(jnp.int32, (256, 256), 1)
    perm = (lj == (252 - (li - lax.rem(li, 4)) + lax.rem(li, 4))).astype(BF16)
    above = jnp.where(rep > 0, latb[0, 16:32, :], 0.0)
    below = jnp.where(rep < 15, latb[1, 0:16, :], 0.0)
    latall = jnp.concatenate([above, latf[...], below], axis=0).astype(BF16)
    latb[2, :, :] = jnp.dot(latall, perm, preferred_element_type=F32)[0:32]
    latb[3, :, :] = jnp.dot(latall, perm, preferred_element_type=F32)[32:64]

    xs = lax.broadcasted_iota(jnp.int32, (64, 128), 0)
    ls = lax.broadcasted_iota(jnp.int32, (64, 128), 1)
    keep = (ls < 12) & ~((ls < 4) & (xs == 63)) & ~((ls >= 8) & (xs == 0))

    def lat_step(b, _):
        rolled = []
        for r in range(8):
            row = latb[2 + r // 4, pl.ds((r % 4) * 8 + b, 1), :]
            skew = pltpu.roll(jnp.broadcast_to(row, (8, 256)), 0, 1, stride=4, stride_axis=0)
            full = [pltpu.roll(skew, 8 + 32 * k, 1)[:, :128] for k in range(8)]
            rolled.append(jnp.where(keep, jnp.concatenate(full, axis=0), 0.0))
        for r in range(6):
            v = rolled[r] + pltpu.roll(rolled[r + 1], 16, 1) + pltpu.roll(rolled[r + 2], 32, 1)
            lat48[b, pl.ds(r * 64, 64), :] = v.astype(BF16)
        return 0

    lax.fori_loop(0, REQ, lat_step, 0)

    def sums(st, b, v):
        f = v[64:320].astype(F32)
        st[pl.ds(b, 1), :] = jnp.sum(f, axis=0, keepdims=True)
        st[pl.ds(8 + b, 1), :] = jnp.sum(f * f, axis=0, keepdims=True)

    def u_step(b, _):
        v = jnp.dot(lat48[b, :, 0:48], wu[...], preferred_element_type=F32).astype(BF16)
        ub[b] = v
        sums(stu.at[0], b, v)
        pltpu.make_async_copy(ub.at[b, pl.ds(64, 256)], u_out.at[b], s_out.at[0, b]).start()
        return 0

    lax.fori_loop(0, REQ, u_step, 0)

    x_event(("L", 0, 0))
    x_event(("R", 0, 0))
    own_chunk(0, 1)

    def stats_send(st, base, k, axis):
        for j in range(1, 4):
            send(st.at[k], st.at[k + j], s_st.at[base + k + j], dev(**{axis: j}), s_stsend.at[base + k + j])

    def stats_sum(st, base, k):
        total = st[k]
        for j in range(1, 4):
            arrived(st.at[k + j], s_st.at[base + k + j])
            total = total + st[k + j]
        return total

    stats_send(stu, 0, 0, "dz")
    x_event(("L", 1, 0))
    x_event(("R", 1, 0))
    own_chunk(1, 1)
    stu[4] = stats_sum(stu, 0, 0)
    yz_event(("L", 0, 0))
    yz_event(("R", 0, 0))
    stats_send(stu, 0, 4, "dy")
    wh_event()
    x_relay(("L", 0, 0))
    x_relay(("L", 1, 0))

    gi = lax.broadcasted_iota(jnp.int32, (CH, CH), 0)
    gj = lax.broadcasted_iota(jnp.int32, (CH, CH), 1)
    gsz = CH // GROUPS
    same = (lax.div(gi, gsz) == lax.div(gj, gsz)).astype(F32)

    def stats_final(st, base):
        total = stats_sum(st, base, 4)
        per = jnp.dot(total, same, preferred_element_type=F32, precision=lax.Precision.HIGHEST)
        per = per * (1.0 / (64 * 64 * gsz))
        m, q = per[0:8], per[8:16]
        st[8, 0:8, :] = m
        st[8, 8:16, :] = lax.rsqrt(q - m * m + EPS)

    pos = lax.broadcasted_iota(jnp.int32, (384, CH), 0)
    col = lax.rem(pos, 64)
    inside = ((pos >= 64) | (rep > 0)) & ((pos < 320) | (rep < 15))

    def normed(v, st, b, gain):
        m = st[8, pl.ds(b, 1), :]
        s = st[8, pl.ds(8 + b, 1), :] * gain
        n = (v.astype(F32) - m) * s
        n = n / (1.0 + jnp.exp(-n))
        n = jnp.where(inside, n, 0.0)
        left = jnp.where(col == 0, 0.0, pltpu.roll(n, 1, 0))
        right = jnp.where(col == 63, 0.0, pltpu.roll(n, 383, 0))
        return left, n, right

    x_event(("L", 0, 1))
    x_event(("R", 0, 1))
    x_relay(("R", 0, 1))
    stats_final(stu, 0)

    def m_step(b, _):
        for i, v in enumerate(normed(ub[b], stu, b, ugain[...].astype(F32))):
            mb[b, i] = v.astype(BF16)
        return 0

    lax.fori_loop(0, REQ, m_step, 0)

    loads[2].wait()

    def conv_step(b):
        acc = ub[b, 64:320, :].astype(F32)
        for i in range(3):
            for j in range(3):
                acc = acc + jnp.dot(
                    mb[b, j, pl.ds(i * 64, 256), :], ucv[i, j], preferred_element_type=F32
                )
        tb[b] = acc
        pltpu.make_async_copy(tb.at[b], t_out.at[b], s_out.at[2, b]).start()

    after = {
        0: [lambda: yz_event(("L", 1, 0)), lambda: yz_event(("R", 1, 0))],
        1: [lambda: x_event(("L", 1, 1)), lambda: x_event(("R", 1, 1)), lambda: x_relay(("R", 1, 1)), own_e2],
        3: [lambda: yz_event(("L", 0, 1)), lambda: yz_event(("R", 0, 1))],
        5: [wh_far],
    }

    def loop_a(b, _):
        conv_step(b)
        for k, todo in after.items():
            @pl.when(b == k)
            def _():
                for f in todo:
                    f()
        return 0

    lax.fori_loop(0, REQ, loop_a, 0)

    loads[1].wait()
    own_wh.wait()
    for i in range(2, 4):
        arrived(hintb.at[:, 0], s_halo.at[i])

    def h_step(b, _):
        n = ids[b, 0]
        w = whs[n]
        v = jnp.dot(hintb[b].reshape(384, 192), w[0:192], preferred_element_type=F32)
        v = v + jnp.dot(lat48[b, :, 0:48], w[192:240], preferred_element_type=F32)
        v = v.astype(BF16)
        hb[b] = v
        sums(sth.at[0], b, v)
        pltpu.make_async_copy(hb.at[b, pl.ds(64, 256)], h_out.at[b], s_out.at[1, b]).start()
        return 0

    lax.fori_loop(0, REQ, h_step, 0)

    x_event(("LL", 0))
    x_event(("RR", 0))
    stats_send(sth, 8, 0, "dz")
    yz_event(("L", 1, 1))
    yz_event(("R", 1, 1))
    sth[4] = stats_sum(sth, 8, 0)
    x_event(("LL", 1))
    x_event(("RR", 1))
    stats_send(sth, 8, 4, "dy")
    e2_event()
    stats_final(sth, 8)

    def n_step(b, _):
        n = ids[b, 0]
        gain = whs[n, 240:256, :][0:1].astype(F32)
        parts = [v.astype(BF16) for v in normed(hb[b], sth, b, gain)]
        for i, v in enumerate(parts):
            nmb[b, i] = v[:, 0:256]
        ntb[b] = jnp.concatenate([v[:, 256:320] for v in parts], axis=1)
        pltpu.make_async_copy(nmb.at[b], nm_out.at[b], s_out.at[3, b]).start()
        pltpu.make_async_copy(ntb.at[b], nt_out.at[b], s_out.at[4, b]).start()
        @pl.when(b == 3)
        def _():
            yz_event(("LL", 0))
            yz_event(("RR", 0))
            e2_far()
        return 0

    lax.fori_loop(0, REQ, n_step, 0)
    yz_event(("LL", 1))
    yz_event(("RR", 1))

    arrived(g.at[pl.ds(0, 4)], s_sib)
    arrived(g.at[pl.ds(0, 7)], s_send)
    arrived(whs.at[pl.ds(0, 7)], s_whsend)
    own_blob.wait()
    for i in range(4):
        src = halos[i][0]
        pltpu.make_async_copy(src, src, s_hsend.at[i]).wait()
    for base, st in ((0, stu), (8, sth)):
        for k in (0, 4):
            for j in range(1, 4):
                arrived(st.at[k], s_stsend.at[base + k + j])

    def out_step(b, _):
        outs = (
            (ub.at[b, pl.ds(64, 256)], u_out), (hb.at[b, pl.ds(64, 256)], h_out),
            (tb.at[b], t_out), (nmb.at[b], nm_out), (ntb.at[b], nt_out),
        )
        for i, (src, dst) in enumerate(outs):
            pltpu.make_async_copy(src, dst.at[b], s_out.at[i, b]).wait()
        return 0

    lax.fori_loop(0, REQ, out_step, 0)


def gather_call(ids, latf, hint, wh, wu, blob, ugain, uconv):
    hbm = pl.BlockSpec(memory_space=pl.ANY)
    vm = pl.BlockSpec(memory_space=pltpu.VMEM)
    sm = pl.BlockSpec(memory_space=pltpu.SMEM)
    dma = pltpu.SemaphoreType.DMA
    return pl.pallas_call(
        gather_kernel,
        out_shape=(
            jax.ShapeDtypeStruct((8, ROWS, 256), BF16),
            jax.ShapeDtypeStruct((REQ, 256, CH), F32),
            jax.ShapeDtypeStruct((REQ, 256, CH), BF16),
            jax.ShapeDtypeStruct((REQ, 256, CH), BF16),
            jax.ShapeDtypeStruct((REQ, 3, 384, 256), BF16),
            jax.ShapeDtypeStruct((REQ, 384, 192), BF16),
        ),
        in_specs=[sm, vm, hbm, vm, vm, hbm, vm, hbm],
        out_specs=(hbm,) * 6,
        scratch_shapes=[
            pltpu.VMEM((ROWS, 256), BF16),
            pltpu.VMEM((8, WHR, CH), BF16),
            pltpu.VMEM((REQ, 6, 64, 192), BF16),
            pltpu.VMEM((4, 32, 256), F32),
            pltpu.VMEM((REQ, 384, 128), BF16),
            pltpu.VMEM((REQ, 384, CH), BF16),
            pltpu.VMEM((REQ, 384, CH), BF16),
            pltpu.VMEM((REQ, 3, 384, CH), BF16),
            pltpu.VMEM((REQ, 256, CH), F32),
            pltpu.VMEM((REQ, 3, 384, 256), BF16),
            pltpu.VMEM((REQ, 384, 192), BF16),
            pltpu.VMEM((3, 3, CH, CH), BF16),
            pltpu.VMEM((9, 16, CH), F32),
            pltpu.VMEM((9, 16, CH), F32),
            dma((12,)), dma((48,)), dma((4,)), dma((4,)), dma, dma, dma, dma,
            dma((4,)), dma((4,)), dma((16,)), dma((16,)), dma((5,)), dma((5, REQ)),
        ],
        compiler_params=pltpu.CompilerParams(
            collective_id=0, has_side_effects=True, vmem_limit_bytes=60 << 20
        ),
        name="gather",
    )(ids, latf, hint, wh, wu, blob, ugain, uconv)


def control_kernel(ids, scale, valid, wb, nm, nt, hb, ub, tb, o0, o1):
    b = pl.program_id(0)
    w = scale[b] * valid[b].astype(F32)

    def dot(a, k):
        return jnp.dot(a, k, preferred_element_type=F32)

    def proj(h, zm, lane, ktail):
        ha, hc, ht = h[:, 0:128], h[:, 128:256], h[:, 256:320]
        main = dot(h[:, 0:256], wb[0, zm : zm + 256, :]) + dot(ht, wb[0, zm + 256 : zm + 320, :])
        zt = wb[0, O_ZT : O_ZT + 128, :]
        tail = dot(ha, zt[:, lane : lane + 64]) + dot(hc, zt[:, 128 + lane : 192 + lane]) + dot(ht, ktail)
        return jnp.concatenate([main, tail], axis=1).astype(BF16).astype(F32)

    h0 = hb[0]
    r0 = proj(h0, O_Z0, 0, wb[0, O_N + 192 : O_N + 256, 192:256])
    o0[0] = (ub[0].astype(F32) + w * r0).astype(BF16).reshape(4, 64, CH)

    main = jnp.zeros((256, 256), F32)
    side = jnp.zeros((256, 192), F32)
    tail = jnp.zeros((256, 64), F32)
    for i in range(3):
        rows = slice(i * 64, i * 64 + 256)
        for j in range(3):
            k = O_M + (i * 3 + j) * 256
            main = main + dot(nm[0, j, rows, :], wb[0, k : k + 256, :])
        k, n = O_K + i * 192, O_N + i * 256
        main = main + dot(nt[0, rows, :], wb[0, k : k + 192, :])
        side = side + dot(nm[0, 1, rows, :], wb[0, n : n + 256, 0:192])
        tail = tail + dot(nt[0, rows, :], wb[0, n : n + 192, 192:256])
    col = lax.rem(lax.broadcasted_iota(jnp.int32, (256, 64), 0), 64)
    left = jnp.where(col == 0, 0.0, pltpu.roll(side[:, 0:64], 1, 0))
    right = jnp.where(col == 63, 0.0, pltpu.roll(side[:, 128:192], 255, 0))
    tail = tail + left + side[:, 64:128] + right
    h1 = (h0.astype(F32) + jnp.concatenate([main, tail], axis=1)).astype(BF16)
    r1 = proj(h1, O_Z1, 64, wb[0, O_N + 448 : O_N + 512, 192:256])
    o1[0] = (tb[0] + w * r1).astype(BF16).reshape(4, 64, CH)


def control_call(ids, scale, valid, g, nm, nt, hb, ub, tb):
    def mine(shape):
        zeros = (0,) * (len(shape) - 1)
        return pl.BlockSpec(shape, lambda b, *_: (b,) + zeros)

    out = jax.ShapeDtypeStruct((REQ, 4, 64, CH), BF16)
    return pl.pallas_call(
        control_kernel,
        out_shape=(out, out),
        grid_spec=pltpu.PrefetchScalarGridSpec(
            num_scalar_prefetch=3,
            grid=(REQ,),
            in_specs=[
                pl.BlockSpec((1, ROWS, 256), lambda b, ids, *_: (ids[b], 0, 0)),
                mine((1, 3, 384, 256)),
                mine((1, 384, 192)),
                mine((1, 256, CH)),
                mine((1, 256, CH)),
                mine((1, 256, CH)),
            ],
            out_specs=[mine((1, 4, 64, CH)), mine((1, 4, 64, CH))],
        ),
        compiler_params=pltpu.CompilerParams(
            dimension_semantics=("arbitrary",), vmem_limit_bytes=60 << 20
        ),
        name="control",
    )(ids, scale, valid, g, nm, nt, hb, ub, tb)


def input_rows(w):
    w = jnp.flip(w, axis=1).reshape(3, 12, CH)
    return jnp.pad(w, ((0, 0), (0, 4), (0, 0))).reshape(48, CH)


def pack(conv, z0, z1):
    m, t = slice(0, 256), slice(256, CH)
    wm = conv[:, :, m, m].reshape(2304, 256)
    wk = conv[:, :, t, m].reshape(576, 256)
    wn = conv[:, :, m, t].transpose(0, 2, 1, 3).reshape(3, 256, 192)
    kt = conv[:, :, t, t].reshape(3, 192, 64)
    zk = jnp.stack([z0[t, t], z1[t, t], jnp.zeros((64, 64), BF16)])
    last = jnp.concatenate([kt, zk], axis=1)
    wn = jnp.concatenate([wn, last], axis=2).reshape(768, 256)
    zt = jnp.concatenate([z0[m, t], z1[m, t]], axis=1).reshape(2, 128, 128)
    zt = jnp.concatenate([zt[0], zt[1]], axis=1)
    return jnp.concatenate([wm, wk, wn, z1[:, m], z0[:, m], zt], axis=0)


def shards(
    latent, hint, cond_ids, valid, cond_scale,
    ctl_in, ctl_hint, ctl_zero0, ctl_gain, ctl_conv, ctl_zero1,
    unet_in, unet_gain, unet_conv,
):
    latf = latent.astype(F32).transpose(1, 0, 2).reshape(32, 256)
    wh = jnp.concatenate(
        [ctl_hint[0], input_rows(ctl_in[0]), ctl_gain, jnp.zeros((15, CH), BF16)], axis=0
    )
    blob = pack(ctl_conv[0], ctl_zero0[0], ctl_zero1[0])
    g, t, u, h, nm, nt = gather_call(
        cond_ids, latf, hint, wh, input_rows(unet_in), blob, unet_gain[None], unet_conv
    )
    return control_call(cond_ids[:, 0], cond_scale, valid, g, nm, nt, h, u, t)


def solution(mesh):
    n, r = "net", "rep"
    return jax.shard_map(
        shards,
        mesh=mesh,
        in_specs=(
            P(n, r, None), P(n, r, None, None), P(n, None), P(n), P(n),
            P(n, None, None, None, None), P(n, None, None), P(n, None, None), P(n, None),
            P(n, None, None, None, None), P(n, None, None), P(), P(), P(),
        ),
        out_specs=(P(n, r, None, None), P(n, r, None, None)),
        check_vma=False,
    )
```

```python
import functools

import jax
import jax.numpy as jnp
from jax import lax
from jax.experimental import pallas as pl
from jax.experimental.pallas import tpu as pltpu
from jax.sharding import PartitionSpec as P

MESH = pl.DeviceIdType.MESH
F32, BF16 = jnp.float32, jnp.bfloat16
CH = 320
GROUPS = 32
REQ = 8
EPS = 1e-5
O_M, O_K, O_N, O_Z1, O_Z0, O_ZT, ROWS = 0, 2304, 2880, 3648, 3968, 4288, 4416
CHUNK = 256
E2 = 16 * CHUNK
E2N = ROWS - E2
E2H = E2N // 2
WHR = 256


def gray(v):
    return v + lax.div(v, 2) - 2 * lax.div(v, 3)


def gather_kernel(
    ids, lat, hint, cin, chint, cgain, conv, z0, z1, uin, ugain, uconv,
    g, t_out, u_out, h_out, nm_out, nt_out,
    blob, whs, cv, z0v, z1v, wu, hintb, latb, lat48, ub, hb, mb, tb, nmb, ntb, ucv, stu, sth,
    s_x, s_yz, s_e, s_wh, s_sib, s_whsib, s_send, s_whsend,
    s_halo, s_hsend, s_st, s_stsend, s_loc, s_out,
):
    net, rep = lax.axis_index("net"), lax.axis_index("rep")
    x, c = lax.div(net, 2), lax.rem(net, 2)
    y, z = lax.div(rep, 4), lax.rem(rep, 4)

    def dev(dx=0, dy=0, dz=0, dc=0):
        return (
            lax.rem(x + dx, 4) * 2 + lax.rem(c + dc, 2),
            lax.rem(y + dy, 4) * 4 + lax.rem(z + dz, 4),
        )

    def rdev(d):
        return (net, lax.rem(rep + d, 16))

    def colour(q, dy=0, dz=0):
        yy, zz = lax.rem(y + dy, 4), lax.rem(z + dz, 4)
        a, b = (yy, zz) if q == 0 else (zz, yy)
        ga, odd = gray(a), lax.rem(b, 2)
        return ga + odd * (3 - 2 * ga)

    def net_of(dx):
        return lax.rem(x + dx, 4) * 2 + c

    barrier = pltpu.get_barrier_semaphore()
    partners = [
        dev(dx=1), dev(dx=3), dev(dc=1), dev(dy=1), dev(dy=3), dev(dy=2),
        dev(dz=1), dev(dz=3), dev(dz=2), rdev(1), rdev(15),
    ]
    for p in partners:
        pl.semaphore_signal(barrier, inc=1, device_id=p, device_id_type=MESH)

    loads = [
        pltpu.make_async_copy(conv.at[0], cv, s_loc.at[0]),
        pltpu.make_async_copy(z0.at[0], z0v, s_loc.at[1]),
        pltpu.make_async_copy(z1.at[0], z1v, s_loc.at[2]),
        pltpu.make_async_copy(chint.at[0], whs.at[net, pl.ds(0, 192)], s_loc.at[3]),
        pltpu.make_async_copy(hint, hintb.at[:, pl.ds(1, 4)], s_loc.at[4]),
        pltpu.make_async_copy(uconv, ucv, s_loc.at[5]),
    ]
    for cp in loads:
        cp.start()

    def input_rows(block):
        parts = [block[i].astype(F32) for i in (2, 1, 0)] + [jnp.zeros((4, CH), F32)]
        return jnp.concatenate(parts, axis=0).astype(BF16)

    for i in range(3):
        whs[net, 192 + 16 * i : 208 + 16 * i, :] = input_rows(cin[0, i])
        wu[16 * i : 16 * i + 16, :] = input_rows(uin[i])
    whs[net, 240:256, :] = jnp.broadcast_to(cgain[...].astype(F32), (16, CH)).astype(BF16)

    for cp in loads[:3]:
        cp.wait()
    for i in range(3):
        for j in range(3):
            k = i * 3 + j
            blob[O_M + k * 256 : O_M + k * 256 + 256, :] = cv[i, j, 0:256, 0:256]
            blob[O_K + k * 64 : O_K + k * 64 + 64, :] = cv[i, j, 256:CH, 0:256]
        n = O_N + i * 256
        if i < 2:
            zk = (z0v, z1v)[i][256:CH, 256:CH]
        else:
            zk = jnp.zeros((64, 64), BF16)
        kt = jnp.concatenate([cv[i, j, 256:CH, 256:CH] for j in range(3)] + [zk], axis=0)
        nt = [cv[i, j, 0:256, 256:CH] for j in range(3)]
        blob[n : n + 256, :] = jnp.concatenate(nt + [kt], axis=1)
    blob[O_Z1 : O_Z1 + CH, :] = z1v[:, 0:256]
    blob[O_Z0 : O_Z0 + CH, :] = z0v[:, 0:256]
    zt = [zv[k : k + 128, 256:CH] for k in (0, 128) for zv in (z0v, z1v)]
    blob[O_ZT : O_ZT + 128, :] = jnp.concatenate(zt, axis=1)
    loads[3].wait()

    pl.semaphore_wait(barrier, len(partners))

    def send(src, dst, sem, where, ssem):
        pltpu.make_async_remote_copy(
            src_ref=src, dst_ref=dst, send_sem=ssem, recv_sem=sem,
            device_id=where, device_id_type=MESH,
        ).start()

    def arrived(ref, sem):
        pltpu.make_async_copy(ref, ref, sem).wait()

    EV = {}
    for q in range(2):
        for h in range(2):
            EV["L", q, h] = (3, q, h, q * 2 + h)
            EV["R", q, h] = (1, q, h, 4 + q * 2 + h)
        EV["LL", q] = (2, q, 0, 8 + q)
        EV["RR", q] = (2, q, 1, 10 + q)

    def rows_of(q, h, dy=0, dz=0):
        start = pl.multiple_of((colour(q, dy, dz) * 2 + (q * 8 + h)) * CHUNK, CHUNK)
        return pl.ds(start, CHUNK)

    def own_chunk(q, h):
        r = rows_of(q, h)
        send(blob.at[r], g.at[net, r], s_x.at[EV["L", q, h][3]], dev(dx=1), s_send)
        send(blob.at[r], g.at[net, r], s_x.at[EV["R", q, h][3]], dev(dx=3), s_send)

    def x_relay(key):
        dx, q, h, _ = EV[key]
        ref = g.at[net_of(dx), rows_of(q, h)]
        if key[0] == "L":
            send(ref, ref, s_x.at[EV["LL", q][3]], dev(dx=1), s_send)
        else:
            send(ref, ref, s_x.at[EV["RR", q][3]], dev(dx=3), s_send)

    def to_sib(ref):
        send(ref, ref, s_sib, dev(dc=1), s_send)

    def dirs(q, h):
        main, other = ((0, 1), (2, 3)) if q == 0 else ((2, 3), (0, 1))
        return main + (other[h],)

    STEP = [dict(dy=1), dict(dy=3), dict(dz=1), dict(dz=3)]
    BACK = [dict(dy=3), dict(dy=1), dict(dz=3), dict(dz=1)]

    def x_event(key):
        dx, q, h, sem = EV[key]
        ref = g.at[net_of(dx), rows_of(q, h)]
        arrived(ref, s_x.at[sem])
        for d in dirs(q, h):
            send(ref, ref, s_yz.at[d * 12 + sem], dev(**STEP[d]), s_send)
        to_sib(ref)

    def yz_event(key):
        dx, q, h, sem = EV[key]
        for d in dirs(q, h):
            ref = g.at[net_of(dx), rows_of(q, h, **BACK[d])]
            arrived(ref, s_yz.at[d * 12 + sem])
            to_sib(ref)

    e2r, e2h = pl.ds(E2, E2N), (pl.ds(E2, E2H), pl.ds(E2 + E2H, E2H))

    def own_e2():
        send(blob.at[e2r], g.at[net, e2r], s_e.at[0], dev(dx=1), s_send)
        send(blob.at[e2r], g.at[net, e2r], s_e.at[1], dev(dx=3), s_send)

    def e2_event():
        for i, dx, to in ((0, 3, 1), (1, 1, 3)):
            ref = g.at[net_of(dx), e2r]
            arrived(ref, s_e.at[i])
            half = g.at[net_of(dx), e2h[i]]
            send(half, half, s_e.at[2 + i], dev(dx=to), s_send)
            to_sib(ref)

    def e2_far():
        for i in range(2):
            ref = g.at[net_of(2), e2h[i]]
            arrived(ref, s_e.at[2 + i])
            to_sib(ref)

    whh = (pl.ds(0, WHR // 2), pl.ds(WHR // 2, WHR // 2))

    def wh_sib(ref):
        send(ref, ref, s_whsib, dev(dc=1), s_whsend)

    def wh_event():
        for i, dx, to in ((0, 3, 1), (1, 1, 3)):
            ref = whs.at[net_of(dx)]
            arrived(ref, s_wh.at[i])
            half = whs.at[net_of(dx), whh[i]]
            send(half, half, s_wh.at[2 + i], dev(dx=to), s_whsend)
            wh_sib(ref)

    def wh_far():
        for i in range(2):
            ref = whs.at[net_of(2), whh[i]]
            arrived(ref, s_wh.at[2 + i])
            wh_sib(ref)
        arrived(whs.at[pl.ds(0, 4)], s_whsib)

    halos = [
        (lat, latb.at[0], rdev(1)), (lat, latb.at[1], rdev(15)),
        (hint.at[:, 3], hintb.at[:, 0], rdev(1)), (hint.at[:, 0], hintb.at[:, 5], rdev(15)),
    ]
    for i, (src, dst, to) in enumerate(halos[:2]):
        send(src, dst, s_halo.at[i], to, s_hsend.at[i])
    own_chunk(0, 0)
    own_chunk(1, 0)
    mine = whs.at[net]
    send(mine, mine, s_wh.at[0], dev(dx=1), s_whsend)
    send(mine, mine, s_wh.at[1], dev(dx=3), s_whsend)
    send(mine, mine, s_whsib, dev(dc=1), s_whsend)
    send(blob, g.at[net], s_sib, dev(dc=1), s_send)
    for i, (src, dst, to) in enumerate(halos):
        if i >= 2:
            send(src, dst, s_halo.at[i], to, s_hsend.at[i])
    own_blob = pltpu.make_async_copy(blob, g.at[net], s_loc.at[6])
    own_blob.start()

    for i in range(2):
        arrived(latb.at[i], s_halo.at[i])
    li = lax.broadcasted_iota(jnp.int32, (256, 256), 0)
    lj = lax.broadcasted_iota(jnp.int32, (256, 256), 1)
    perm = (lj == (252 - (li - lax.rem(li, 4)) + lax.rem(li, 4))).astype(BF16)
    xs = lax.broadcasted_iota(jnp.int32, (64, 128), 0)
    ls = lax.broadcasted_iota(jnp.int32, (64, 128), 1)
    keep = (ls < 12) & ~((ls < 4) & (xs == 63)) & ~((ls >= 8) & (xs == 0))

    def lat_step(b, _):
        rolled = []
        above = jnp.where(rep > 0, latb[0, b].astype(F32)[2:4], 0.0)
        below = jnp.where(rep < 15, latb[1, b].astype(F32)[0:2], 0.0)
        rows = jnp.concatenate([above, lat[b].astype(F32), below], axis=0).astype(BF16)
        rows = jnp.dot(rows, perm, preferred_element_type=F32)
        for r in range(8):
            row = rows[r : r + 1]
            skew = pltpu.roll(jnp.broadcast_to(row, (8, 256)), 0, 1, stride=4, stride_axis=0)
            full = [pltpu.roll(skew, 8 + 32 * k, 1)[:, :128] for k in range(8)]
            rolled.append(jnp.where(keep, jnp.concatenate(full, axis=0), 0.0))
        for r in range(6):
            v = rolled[r] + pltpu.roll(rolled[r + 1], 16, 1) + pltpu.roll(rolled[r + 2], 32, 1)
            lat48[b, pl.ds(r * 64, 64), :] = v.astype(BF16)
        return 0

    lax.fori_loop(0, REQ, lat_step, 0)

    def sums(st, b, v):
        f = v[64:320].astype(F32)
        st[pl.ds(b, 1), :] = jnp.sum(f, axis=0, keepdims=True)
        st[pl.ds(8 + b, 1), :] = jnp.sum(f * f, axis=0, keepdims=True)

    def u_step(b, _):
        v = jnp.dot(lat48[b, :, 0:48], wu[...], preferred_element_type=F32).astype(BF16)
        ub[b] = v
        sums(stu.at[0], b, v)
        pltpu.make_async_copy(ub.at[b, pl.ds(64, 256)], u_out.at[b], s_out.at[0, b]).start()
        return 0

    lax.fori_loop(0, REQ, u_step, 0)

    def stats_send(st, base, k, axis):
        for j in range(1, 4):
            send(st.at[k], st.at[k + j], s_st.at[base + k + j], dev(**{axis: j}), s_stsend.at[base + k + j])

    def stats_sum(st, base, k):
        total = st[k]
        for j in range(1, 4):
            arrived(st.at[k + j], s_st.at[base + k + j])
            total = total + st[k + j]
        return total

    stats_send(stu, 0, 0, "dz")
    x_event(("L", 0, 0))
    x_event(("R", 0, 0))
    own_chunk(0, 1)
    stu[4] = stats_sum(stu, 0, 0)
    x_event(("L", 1, 0))
    stats_send(stu, 0, 4, "dy")
    x_event(("R", 1, 0))
    own_chunk(1, 1)

    gi = lax.broadcasted_iota(jnp.int32, (CH, CH), 0)
    gj = lax.broadcasted_iota(jnp.int32, (CH, CH), 1)
    gsz = CH // GROUPS
    same = (lax.div(gi, gsz) == lax.div(gj, gsz)).astype(F32)

    def stats_final(st, base):
        total = stats_sum(st, base, 4)
        per = jnp.dot(total, same, preferred_element_type=F32, precision=lax.Precision.HIGHEST)
        per = per * (1.0 / (64 * 64 * gsz))
        m, q = per[0:8], per[8:16]
        st[8, 0:8, :] = m
        st[8, 8:16, :] = lax.rsqrt(q - m * m + EPS)

    pos = lax.broadcasted_iota(jnp.int32, (384, CH), 0)
    col = lax.rem(pos, 64)
    inside = ((pos >= 64) | (rep > 0)) & ((pos < 320) | (rep < 15))

    def normed(v, st, b, gain):
        m = st[8, pl.ds(b, 1), :]
        s = st[8, pl.ds(8 + b, 1), :] * gain
        n = (v.astype(F32) - m) * s
        n = n / (1.0 + jnp.exp(-n))
        n = jnp.where(inside, n, 0.0)
        left = jnp.where(col == 0, 0.0, pltpu.roll(n, 1, 0))
        right = jnp.where(col == 63, 0.0, pltpu.roll(n, 383, 0))
        return left, n, right

    def run(todo):
        for name, key in todo:
            if name == "x":
                x_event(key)
            elif name == "yz":
                yz_event(key)
            elif name == "relay":
                x_relay(key)
            else:
                key()

    def loop(first, last, piece, after):
        def body(b, _):
            piece(b)
            for k, todo in after.items():
                @pl.when(b == k)
                def _():
                    run(todo)
            return 0

        lax.fori_loop(first, last, body, 0)

    run([("yz", ("L", 0, 0))])
    stats_final(stu, 0)

    def m_step(b):
        for i, v in enumerate(normed(ub[b], stu, b, ugain[...].astype(F32).reshape(1, CH))):
            mb[b, i] = v.astype(BF16)

    loop(0, REQ, m_step, {
        2: [("yz", ("R", 0, 0))],
        4: [("wh", wh_event), ("relay", ("L", 0, 0)), ("relay", ("L", 1, 0))],
        7: [("yz", ("L", 1, 0))],
    })

    loads[5].wait()

    def conv_step(b):
        acc = ub[b, 64:320, :].astype(F32)
        for i in range(3):
            for j in range(3):
                acc = acc + jnp.dot(
                    mb[b, j, pl.ds(i * 64, 256), :], ucv[i, j], preferred_element_type=F32
                )
        tb[b] = acc
        pltpu.make_async_copy(tb.at[b], t_out.at[b], s_out.at[2, b]).start()

    loop(0, 5, conv_step, {
        0: [("x", ("L", 0, 1)), ("x", ("R", 0, 1)), ("relay", ("R", 0, 1))],
        1: [("yz", ("R", 1, 0))],
        2: [("x", ("L", 1, 1)), ("x", ("R", 1, 1)), ("relay", ("R", 1, 1)), ("e2", own_e2)],
        3: [("yz", ("L", 0, 1))],
    })
    wh_far()

    loads[4].wait()
    for i in range(2, 4):
        arrived(hintb.at[:, 0], s_halo.at[i])

    def h_step(b):
        n = ids[b]
        w = whs[n]
        v = jnp.dot(hintb[b].reshape(384, 192), w[0:192], preferred_element_type=F32)
        v = v + jnp.dot(lat48[b, :, 0:48], w[192:240], preferred_element_type=F32)
        v = v.astype(BF16)
        hb[b] = v
        sums(sth.at[0], b, v)
        pltpu.make_async_copy(hb.at[b, pl.ds(64, 256)], h_out.at[b], s_out.at[1, b]).start()

    loop(0, REQ, h_step, {4: [("yz", ("R", 0, 1))]})
    stats_send(sth, 8, 0, "dz")
    run([("x", ("LL", 0)), ("x", ("RR", 0))])

    def stats_turn():
        sth[4] = stats_sum(sth, 8, 0)

    loop(5, REQ, conv_step, {
        5: [("yz", ("L", 1, 1)), ("stats", stats_turn)],
        6: [("x", ("LL", 1)), ("x", ("RR", 1))],
        7: [("yz", ("R", 1, 1))],
    })
    stats_send(sth, 8, 4, "dy")
    e2_event()
    run([("yz", ("LL", 0))])
    stats_final(sth, 8)

    def n_step(b):
        n = ids[b]
        gain = whs[n, 240:256, :][0:1].astype(F32)
        parts = [v.astype(BF16) for v in normed(hb[b], sth, b, gain)]
        for i, v in enumerate(parts):
            nmb[b, i] = v[:, 0:256]
        ntb[b] = jnp.concatenate([v[:, 256:320] for v in parts], axis=1)
        pltpu.make_async_copy(nmb.at[b], nm_out.at[b], s_out.at[3, b]).start()
        pltpu.make_async_copy(ntb.at[b], nt_out.at[b], s_out.at[4, b]).start()

    loop(0, REQ, n_step, {
        2: [("yz", ("RR", 0))],
        5: [("e2", e2_far), ("yz", ("LL", 1))],
    })
    run([("yz", ("RR", 1))])

    arrived(g.at[pl.ds(0, 4)], s_sib)
    arrived(g.at[pl.ds(0, 7)], s_send)
    arrived(whs.at[pl.ds(0, 7)], s_whsend)
    own_blob.wait()
    for i in range(4):
        src = halos[i][0]
        pltpu.make_async_copy(src, src, s_hsend.at[i]).wait()
    for base, st in ((0, stu), (8, sth)):
        for k in (0, 4):
            for j in range(1, 4):
                arrived(st.at[k], s_stsend.at[base + k + j])

    def out_step(b, _):
        outs = (
            (ub.at[b, pl.ds(64, 256)], u_out), (hb.at[b, pl.ds(64, 256)], h_out),
            (tb.at[b], t_out), (nmb.at[b], nm_out), (ntb.at[b], nt_out),
        )
        for i, (src, dst) in enumerate(outs):
            pltpu.make_async_copy(src, dst.at[b], s_out.at[i, b]).wait()
        return 0

    lax.fori_loop(0, REQ, out_step, 0)


def gather_call(*args):
    hbm = pl.BlockSpec(memory_space=pl.ANY)
    vm = pl.BlockSpec(memory_space=pltpu.VMEM)
    sm = pl.BlockSpec(memory_space=pltpu.SMEM)
    dma = pltpu.SemaphoreType.DMA
    return pl.pallas_call(
        gather_kernel,
        out_shape=(
            jax.ShapeDtypeStruct((8, ROWS, 256), BF16),
            jax.ShapeDtypeStruct((REQ, 256, CH), F32),
            jax.ShapeDtypeStruct((REQ, 256, CH), BF16),
            jax.ShapeDtypeStruct((REQ, 256, CH), BF16),
            jax.ShapeDtypeStruct((REQ, 3, 384, 256), BF16),
            jax.ShapeDtypeStruct((REQ, 384, 192), BF16),
        ),
        in_specs=[sm, vm, hbm, vm, hbm, vm, hbm, hbm, hbm, vm, vm, hbm],
        out_specs=(hbm,) * 6,
        scratch_shapes=[
            pltpu.VMEM((ROWS, 256), BF16),
            pltpu.VMEM((8, WHR, CH), BF16),
            pltpu.VMEM((3, 3, CH, CH), BF16),
            pltpu.VMEM((CH, CH), BF16),
            pltpu.VMEM((CH, CH), BF16),
            pltpu.VMEM((48, CH), BF16),
            pltpu.VMEM((REQ, 6, 64, 192), BF16),
            pltpu.VMEM((2, REQ, 4, 256), BF16),
            pltpu.VMEM((REQ, 384, 128), BF16),
            pltpu.VMEM((REQ, 384, CH), BF16),
            pltpu.VMEM((REQ, 384, CH), BF16),
            pltpu.VMEM((REQ, 3, 384, CH), BF16),
            pltpu.VMEM((REQ, 256, CH), F32),
            pltpu.VMEM((REQ, 3, 384, 256), BF16),
            pltpu.VMEM((REQ, 384, 192), BF16),
            pltpu.VMEM((3, 3, CH, CH), BF16),
            pltpu.VMEM((9, 16, CH), F32),
            pltpu.VMEM((9, 16, CH), F32),
            dma((12,)), dma((48,)), dma((4,)), dma((4,)), dma, dma, dma, dma,
            dma((4,)), dma((4,)), dma((16,)), dma((16,)), dma((7,)), dma((5, REQ)),
        ],
        compiler_params=pltpu.CompilerParams(
            collective_id=0, has_side_effects=True, vmem_limit_bytes=60 << 20
        ),
        name="gather",
    )(*args)


def control_kernel(ids, scale, valid, wb, nm, nt, hb, ub, tb, o0, o1):
    b = pl.program_id(0)
    w = scale[b] * valid[b].astype(F32)

    def dot(a, k):
        return jnp.dot(a, k, preferred_element_type=F32)

    def proj(h, zm, lane, ktail):
        ha, hc, ht = h[:, 0:128], h[:, 128:256], h[:, 256:320]
        main = dot(h[:, 0:256], wb[0, zm : zm + 256, :]) + dot(ht, wb[0, zm + 256 : zm + 320, :])
        zt = wb[0, O_ZT : O_ZT + 128, :]
        tail = dot(ha, zt[:, lane : lane + 64]) + dot(hc, zt[:, 128 + lane : 192 + lane]) + dot(ht, ktail)
        return jnp.concatenate([main, tail], axis=1).astype(BF16).astype(F32)

    h0 = hb[0]
    r0 = proj(h0, O_Z0, 0, wb[0, O_N + 192 : O_N + 256, 192:256])
    o0[0] = (ub[0].astype(F32) + w * r0).astype(BF16).reshape(4, 64, CH)

    main = jnp.zeros((256, 256), F32)
    side = jnp.zeros((256, 192), F32)
    tail = jnp.zeros((256, 64), F32)
    for i in range(3):
        rows = slice(i * 64, i * 64 + 256)
        for j in range(3):
            k = O_M + (i * 3 + j) * 256
            main = main + dot(nm[0, j, rows, :], wb[0, k : k + 256, :])
        k, n = O_K + i * 192, O_N + i * 256
        main = main + dot(nt[0, rows, :], wb[0, k : k + 192, :])
        side = side + dot(nm[0, 1, rows, :], wb[0, n : n + 256, 0:192])
        tail = tail + dot(nt[0, rows, :], wb[0, n : n + 192, 192:256])
    col = lax.rem(lax.broadcasted_iota(jnp.int32, (256, 64), 0), 64)
    left = jnp.where(col == 0, 0.0, pltpu.roll(side[:, 0:64], 1, 0))
    right = jnp.where(col == 63, 0.0, pltpu.roll(side[:, 128:192], 255, 0))
    tail = tail + left + side[:, 64:128] + right
    h1 = (h0.astype(F32) + jnp.concatenate([main, tail], axis=1)).astype(BF16)
    r1 = proj(h1, O_Z1, 64, wb[0, O_N + 448 : O_N + 512, 192:256])
    o1[0] = (tb[0] + w * r1).astype(BF16).reshape(4, 64, CH)


def control_call(ids, scale, valid, g, nm, nt, hb, ub, tb):
    def mine(shape):
        zeros = (0,) * (len(shape) - 1)
        return pl.BlockSpec(shape, lambda b, *_: (b,) + zeros)

    out = jax.ShapeDtypeStruct((REQ, 4, 64, CH), BF16)
    return pl.pallas_call(
        control_kernel,
        out_shape=(out, out),
        grid_spec=pltpu.PrefetchScalarGridSpec(
            num_scalar_prefetch=3,
            grid=(REQ,),
            in_specs=[
                pl.BlockSpec((1, ROWS, 256), lambda b, ids, *_: (ids[b], 0, 0)),
                mine((1, 3, 384, 256)),
                mine((1, 384, 192)),
                mine((1, 256, CH)),
                mine((1, 256, CH)),
                mine((1, 256, CH)),
            ],
            out_specs=[mine((1, 4, 64, CH)), mine((1, 4, 64, CH))],
        ),
        compiler_params=pltpu.CompilerParams(
            dimension_semantics=("arbitrary",), vmem_limit_bytes=60 << 20
        ),
        name="control",
    )(ids, scale, valid, g, nm, nt, hb, ub, tb)


def shards(
    latent, hint, cond_ids, valid, cond_scale,
    ctl_in, ctl_hint, ctl_zero0, ctl_gain, ctl_conv, ctl_zero1,
    unet_in, unet_gain, unet_conv,
):
    ids = cond_ids[:, 0]
    g, t, u, h, nm, nt = gather_call(
        ids, latent, hint, ctl_in, ctl_hint, ctl_gain, ctl_conv, ctl_zero0, ctl_zero1,
        unet_in, unet_gain, unet_conv,
    )
    return control_call(ids, cond_scale, valid, g, nm, nt, h, u, t)


def solution(mesh):
    n, r = "net", "rep"
    return jax.shard_map(
        shards,
        mesh=mesh,
        in_specs=(
            P(n, r, None), P(n, r, None, None), P(n, None), P(n), P(n),
            P(n, None, None, None, None), P(n, None, None), P(n, None, None), P(n, None),
            P(n, None, None, None, None), P(n, None, None), P(), P(), P(),
        ),
        out_specs=(P(n, r, None, None), P(n, r, None, None)),
        check_vma=False,
    )
```

```python
import functools

import jax
import jax.numpy as jnp
from jax import lax
from jax.experimental import pallas as pl
from jax.experimental.pallas import tpu as pltpu
from jax.sharding import PartitionSpec as P

MESH = pl.DeviceIdType.MESH
F32, BF16 = jnp.float32, jnp.bfloat16
CH = 320
GROUPS = 32
REQ = 8
EPS = 1e-5
O_M, O_K, O_N, O_Z1, O_Z0, O_ZT, ROWS = 0, 2304, 2880, 3648, 3968, 4288, 4416
CHUNK = 224
E2 = 16 * CHUNK
E2N = ROWS - E2
E2H = E2N // 2
WHR = 256


def gray(v):
    return v + lax.div(v, 2) - 2 * lax.div(v, 3)


def gather_kernel(
    ids, lat, hint, cin, chint, cgain, conv, z0, z1, uin, ugain, uconv,
    g, t_out, u_out, h_out, nm_out, nt_out,
    blob, whs, cv, z0v, z1v, wu, hintb, latb, lat48, ub, hb, mb, tb, nmb, ntb, ucv, raw, st, fin,
    s_x, s_yz, s_e, s_wh, s_sib, s_whsib, s_send, s_whsend,
    s_halo, s_hsend, s_st, s_stsend, s_loc, s_out,
):
    net, rep = lax.axis_index("net"), lax.axis_index("rep")
    x, c = lax.div(net, 2), lax.rem(net, 2)
    y, z = lax.div(rep, 4), lax.rem(rep, 4)

    def dev(dx=0, dy=0, dz=0, dc=0):
        return (
            lax.rem(x + dx, 4) * 2 + lax.rem(c + dc, 2),
            lax.rem(y + dy, 4) * 4 + lax.rem(z + dz, 4),
        )

    def rdev(d):
        return (net, lax.rem(rep + d, 16))

    def colour(q, dy=0, dz=0):
        yy, zz = lax.rem(y + dy, 4), lax.rem(z + dz, 4)
        a, b = (yy, zz) if q == 0 else (zz, yy)
        ga, odd = gray(a), lax.rem(b, 2)
        return ga + odd * (3 - 2 * ga)

    def net_of(dx):
        return lax.rem(x + dx, 4) * 2 + c

    barrier = pltpu.get_barrier_semaphore()
    partners = [
        dev(dx=1), dev(dx=3), dev(dc=1), dev(dy=1), dev(dy=3), dev(dy=2),
        dev(dz=1), dev(dz=3), dev(dz=2), rdev(1), rdev(15),
    ]
    for p in partners:
        pl.semaphore_signal(barrier, inc=1, device_id=p, device_id_type=MESH)

    loads = [
        pltpu.make_async_copy(conv.at[0], cv, s_loc.at[0]),
        pltpu.make_async_copy(z0.at[0], z0v, s_loc.at[1]),
        pltpu.make_async_copy(z1.at[0], z1v, s_loc.at[2]),
        pltpu.make_async_copy(chint.at[0], whs.at[net, pl.ds(0, 192)], s_loc.at[3]),
        pltpu.make_async_copy(hint, hintb.at[:, pl.ds(1, 4)], s_loc.at[4]),
        pltpu.make_async_copy(uconv, ucv, s_loc.at[5]),
    ]
    for cp in loads:
        cp.start()

    def input_rows(block):
        parts = [block[i].astype(F32) for i in (2, 1, 0)] + [jnp.zeros((4, CH), F32)]
        return jnp.concatenate(parts, axis=0).astype(BF16)

    for i in range(3):
        whs[net, 192 + 16 * i : 208 + 16 * i, :] = input_rows(cin[0, i])
        wu[16 * i : 16 * i + 16, :] = input_rows(uin[i])
    whs[net, 240:256, :] = jnp.broadcast_to(cgain[...].astype(F32), (16, CH)).astype(BF16)

    loads[3].wait()

    pl.semaphore_wait(barrier, len(partners))

    def send(src, dst, sem, where, ssem):
        pltpu.make_async_remote_copy(
            src_ref=src, dst_ref=dst, send_sem=ssem, recv_sem=sem,
            device_id=where, device_id_type=MESH,
        ).start()

    def arrived(ref, sem):
        pltpu.make_async_copy(ref, ref, sem).wait()

    EV = {}
    for q in range(2):
        for h in range(2):
            EV["L", q, h] = (3, q, h, q * 2 + h)
            EV["R", q, h] = (1, q, h, 4 + q * 2 + h)
        EV["LL", q] = (2, q, 0, 8 + q)
        EV["RR", q] = (2, q, 1, 10 + q)

    def rows_of(q, h, dy=0, dz=0):
        start = pl.multiple_of((colour(q, dy, dz) * 2 + (q * 8 + h)) * CHUNK, CHUNK)
        return pl.ds(start, CHUNK)

    def own_chunk(q, h):
        r = rows_of(q, h)
        send(blob.at[r], g.at[net, r], s_x.at[EV["L", q, h][3]], dev(dx=1), s_send)
        send(blob.at[r], g.at[net, r], s_x.at[EV["R", q, h][3]], dev(dx=3), s_send)

    def x_relay(key):
        dx, q, h, _ = EV[key]
        ref = g.at[net_of(dx), rows_of(q, h)]
        if key[0] == "L":
            send(ref, ref, s_x.at[EV["LL", q][3]], dev(dx=1), s_send)
        else:
            send(ref, ref, s_x.at[EV["RR", q][3]], dev(dx=3), s_send)

    def to_sib(ref):
        send(ref, ref, s_sib, dev(dc=1), s_send)

    def dirs(q, h):
        main, other = ((0, 1), (2, 3)) if q == 0 else ((2, 3), (0, 1))
        return main + (other[h],)

    STEP = [dict(dy=1), dict(dy=3), dict(dz=1), dict(dz=3)]
    BACK = [dict(dy=3), dict(dy=1), dict(dz=3), dict(dz=1)]

    def x_event(key):
        dx, q, h, sem = EV[key]
        ref = g.at[net_of(dx), rows_of(q, h)]
        arrived(ref, s_x.at[sem])
        for d in dirs(q, h):
            send(ref, ref, s_yz.at[d * 12 + sem], dev(**STEP[d]), s_send)
        to_sib(ref)

    def yz_event(key):
        dx, q, h, sem = EV[key]
        for d in dirs(q, h):
            ref = g.at[net_of(dx), rows_of(q, h, **BACK[d])]
            arrived(ref, s_yz.at[d * 12 + sem])
            to_sib(ref)

    e2r, e2h = pl.ds(E2, E2N), (pl.ds(E2, E2H), pl.ds(E2 + E2H, E2H))

    def own_e2():
        send(blob.at[e2r], g.at[net, e2r], s_e.at[0], dev(dx=1), s_send)
        send(blob.at[e2r], g.at[net, e2r], s_e.at[1], dev(dx=3), s_send)

    def e2_event():
        for i, dx, to in ((0, 3, 1), (1, 1, 3)):
            ref = g.at[net_of(dx), e2r]
            arrived(ref, s_e.at[i])
            half = g.at[net_of(dx), e2h[i]]
            send(half, half, s_e.at[2 + i], dev(dx=to), s_send)
            to_sib(ref)

    def e2_far():
        for i in range(2):
            ref = g.at[net_of(2), e2h[i]]
            arrived(ref, s_e.at[2 + i])
            to_sib(ref)

    whh = (pl.ds(0, WHR // 2), pl.ds(WHR // 2, WHR // 2))

    def wh_sib(ref):
        send(ref, ref, s_whsib, dev(dc=1), s_whsend)

    def wh_event():
        for i, dx, to in ((0, 3, 1), (1, 1, 3)):
            ref = whs.at[net_of(dx)]
            arrived(ref, s_wh.at[i])
            half = whs.at[net_of(dx), whh[i]]
            send(half, half, s_wh.at[2 + i], dev(dx=to), s_whsend)
            wh_sib(ref)

    def wh_far():
        for i in range(2):
            ref = whs.at[net_of(2), whh[i]]
            arrived(ref, s_wh.at[2 + i])
            wh_sib(ref)
        arrived(whs.at[pl.ds(0, 4)], s_whsib)

    halos = [
        (lat, latb.at[0], rdev(1)), (lat, latb.at[1], rdev(15)),
        (hint.at[:, 3], hintb.at[:, 0], rdev(1)), (hint.at[:, 0], hintb.at[:, 5], rdev(15)),
    ]
    for i, (src, dst, to) in enumerate(halos[:2]):
        send(src, dst, s_halo.at[i], to, s_hsend.at[i])
    mine = whs.at[net]
    send(mine, mine, s_wh.at[0], dev(dx=1), s_whsend)
    send(mine, mine, s_wh.at[1], dev(dx=3), s_whsend)
    send(mine, mine, s_whsib, dev(dc=1), s_whsend)
    for i, (src, dst, to) in enumerate(halos):
        if i >= 2:
            send(src, dst, s_halo.at[i], to, s_hsend.at[i])

    for cp in loads[:3]:
        cp.wait()
    for i in range(3):
        for j in range(3):
            k = i * 3 + j
            blob[O_M + k * 256 : O_M + k * 256 + 256, :] = cv[i, j, 0:256, 0:256]
            blob[O_K + k * 64 : O_K + k * 64 + 64, :] = cv[i, j, 256:CH, 0:256]
        n = O_N + i * 256
        if i < 2:
            zk = (z0v, z1v)[i][256:CH, 256:CH]
        else:
            zk = jnp.zeros((64, 64), BF16)
        kt = jnp.concatenate([cv[i, j, 256:CH, 256:CH] for j in range(3)] + [zk], axis=0)
        nt = [cv[i, j, 0:256, 256:CH] for j in range(3)]
        blob[n : n + 256, :] = jnp.concatenate(nt + [kt], axis=1)
    blob[O_Z1 : O_Z1 + CH, :] = z1v[:, 0:256]
    blob[O_Z0 : O_Z0 + CH, :] = z0v[:, 0:256]
    zt = [zv[k : k + 128, 256:CH] for k in (0, 128) for zv in (z0v, z1v)]
    blob[O_ZT : O_ZT + 128, :] = jnp.concatenate(zt, axis=1)
    own_blob = pltpu.make_async_copy(blob, g.at[net], s_loc.at[6])
    own_blob.start()

    def run(todo):
        for name, key in todo:
            if name == "x":
                x_event(key)
            elif name == "yz":
                yz_event(key)
            elif name == "relay":
                x_relay(key)
            elif name == "own":
                own_chunk(*key)
            else:
                key()

    def loop(first, last, piece, after):
        def body(b, _):
            piece(b)
            for k, todo in after.items():
                @pl.when(b == k)
                def _():
                    run(todo)
            return 0

        lax.fori_loop(first, last, body, 0)

    for i in range(2):
        arrived(latb.at[i], s_halo.at[i])
    li = lax.broadcasted_iota(jnp.int32, (256, 256), 0)
    lj = lax.broadcasted_iota(jnp.int32, (256, 256), 1)
    perm = (lj == (252 - (li - lax.rem(li, 4)) + lax.rem(li, 4))).astype(BF16)
    xs = lax.broadcasted_iota(jnp.int32, (64, 128), 0)
    ls = lax.broadcasted_iota(jnp.int32, (64, 128), 1)
    keep = (ls < 12) & ~((ls < 4) & (xs == 63)) & ~((ls >= 8) & (xs == 0))

    def lat_step(b):
        rolled = []
        above = jnp.where(rep > 0, latb[0, b].astype(F32)[2:4], 0.0)
        below = jnp.where(rep < 15, latb[1, b].astype(F32)[0:2], 0.0)
        rows = jnp.concatenate([above, lat[b].astype(F32), below], axis=0).astype(BF16)
        rows = jnp.dot(rows, perm, preferred_element_type=F32)
        for r in range(8):
            row = rows[r : r + 1]
            skew = pltpu.roll(jnp.broadcast_to(row, (8, 256)), 0, 1, stride=4, stride_axis=0)
            full = [pltpu.roll(skew, 8 + 32 * k, 1)[:, :128] for k in range(8)]
            rolled.append(jnp.where(keep, jnp.concatenate(full, axis=0), 0.0))
        for r in range(6):
            v = rolled[r] + pltpu.roll(rolled[r + 1], 16, 1) + pltpu.roll(rolled[r + 2], 32, 1)
            lat48[b, pl.ds(r * 64, 64), :] = v.astype(BF16)

    loop(0, REQ, lat_step, {
        5: [("wh", wh_event)] + [("own", (q, h)) for h in range(2) for q in range(2)],
    })

    def sums(row, v):
        f = v[64:320].astype(F32)
        raw[pl.ds(row, 1), :] = jnp.sum(f, axis=0, keepdims=True)
        raw[pl.ds(8 + row, 1), :] = jnp.sum(f * f, axis=0, keepdims=True)

    def u_step(b, _):
        v = jnp.dot(lat48[b, :, 0:48], wu[...], preferred_element_type=F32).astype(BF16)
        ub[b] = v
        sums(b, v)
        pltpu.make_async_copy(ub.at[b, pl.ds(64, 256)], u_out.at[b], s_out.at[0, b]).start()
        return 0

    lax.fori_loop(0, REQ, u_step, 0)

    wh_far()
    send(blob, g.at[net], s_sib, dev(dc=1), s_send)
    loads[4].wait()
    for i in range(2, 4):
        arrived(hintb.at[:, 0], s_halo.at[i])

    def h_step(b):
        n = ids[b]
        w = whs[n]
        v = jnp.dot(hintb[b].reshape(384, 192), w[0:192], preferred_element_type=F32)
        v = v + jnp.dot(lat48[b, :, 0:48], w[192:240], preferred_element_type=F32)
        v = v.astype(BF16)
        hb[b] = v
        sums(16 + b, v)
        pltpu.make_async_copy(hb.at[b, pl.ds(64, 256)], h_out.at[b], s_out.at[1, b]).start()

    loop(0, REQ, h_step, {})

    def stats_send(k, axis):
        for j in range(1, 4):
            send(st.at[k], st.at[k + j], s_st.at[k + j], dev(**{axis: j}), s_stsend.at[k + j])

    def stats_sum(k):
        total = st[k]
        for j in range(1, 4):
            arrived(st.at[k + j], s_st.at[k + j])
            total = total + st[k + j]
        return total

    gsz = CH // GROUPS
    gi = lax.broadcasted_iota(jnp.int32, (CH, 128), 0)
    gj = lax.broadcasted_iota(jnp.int32, (CH, 128), 1)
    member = (lax.div(gi, gsz) == gj).astype(F32)
    st[0] = jnp.dot(raw[...], member, preferred_element_type=F32, precision=lax.Precision.HIGHEST)
    stats_send(0, "dz")
    st[4] = stats_sum(0)
    stats_send(4, "dy")
    run([("x", ("L", 0, 0)), ("x", ("R", 0, 0)), ("x", ("L", 1, 0)), ("x", ("R", 1, 0))])
    run([("relay", ("L", 0, 0)), ("relay", ("L", 1, 0))])

    per = stats_sum(4) * (1.0 / (64 * 64 * gsz))
    for k in (0, 16):
        m, q = per[k : k + 8], per[k + 8 : k + 16]
        both = jnp.concatenate([m, lax.rsqrt(q - m * m + EPS)], axis=0)
        fin[k : k + 16, :] = lax.dot_general(
            both, member, (((1,), (1,)), ((), ())),
            preferred_element_type=F32, precision=lax.Precision.HIGHEST,
        )

    pos = lax.broadcasted_iota(jnp.int32, (384, CH), 0)
    col = lax.rem(pos, 64)
    inside = ((pos >= 64) | (rep > 0)) & ((pos < 320) | (rep < 15))

    def normed(v, row, gain):
        m = fin[pl.ds(row, 1), :]
        s = fin[pl.ds(8 + row, 1), :] * gain
        n = (v.astype(F32) - m) * s
        n = n / (1.0 + jnp.exp(-n))
        n = jnp.where(inside, n, 0.0)
        left = jnp.where(col == 0, 0.0, pltpu.roll(n, 1, 0))
        right = jnp.where(col == 63, 0.0, pltpu.roll(n, 383, 0))
        return left, n, right

    def m_step(b):
        for i, v in enumerate(normed(ub[b], b, ugain[...].astype(F32).reshape(1, CH))):
            mb[b, i] = v.astype(BF16)

    loop(0, REQ, m_step, {
        1: [("x", ("L", 0, 1)), ("x", ("R", 0, 1)), ("relay", ("R", 0, 1))],
        3: [("yz", ("L", 0, 0))],
        5: [("x", ("L", 1, 1)), ("x", ("R", 1, 1)), ("relay", ("R", 1, 1)), ("e2", own_e2)],
        7: [("yz", ("R", 0, 0))],
    })

    loads[5].wait()

    def conv_step(b):
        acc = ub[b, 64:320, :].astype(F32)
        for i in range(3):
            for j in range(3):
                acc = acc + jnp.dot(
                    mb[b, j, pl.ds(i * 64, 256), :], ucv[i, j], preferred_element_type=F32
                )
        tb[b] = acc
        pltpu.make_async_copy(tb.at[b], t_out.at[b], s_out.at[2, b]).start()

    loop(0, REQ, conv_step, {
        0: [("yz", ("L", 1, 0))],
        1: [("x", ("LL", 0)), ("x", ("RR", 0))],
        2: [("x", ("LL", 1)), ("x", ("RR", 1))],
        3: [("yz", ("R", 1, 0))],
        5: [("yz", ("L", 0, 1)), ("yz", ("L", 1, 1))],
        7: [("yz", ("R", 0, 1)), ("yz", ("R", 1, 1))],
    })

    def n_step(b):
        n = ids[b]
        gain = whs[n, 240:256, :][0:1].astype(F32)
        parts = [v.astype(BF16) for v in normed(hb[b], 16 + b, gain)]
        for i, v in enumerate(parts):
            nmb[b, i] = v[:, 0:256]
        ntb[b] = jnp.concatenate([v[:, 256:320] for v in parts], axis=1)
        pltpu.make_async_copy(nmb.at[b], nm_out.at[b], s_out.at[3, b]).start()
        pltpu.make_async_copy(ntb.at[b], nt_out.at[b], s_out.at[4, b]).start()

    loop(0, REQ, n_step, {7: [("yz", ("LL", 0))]})
    e2_event()
    run([("yz", ("RR", 0)), ("yz", ("LL", 1)), ("yz", ("RR", 1))])
    e2_far()

    arrived(g.at[pl.ds(0, 4)], s_sib)
    arrived(g.at[pl.ds(0, 7)], s_send)
    arrived(whs.at[pl.ds(0, 7)], s_whsend)
    own_blob.wait()
    for i in range(4):
        src = halos[i][0]
        pltpu.make_async_copy(src, src, s_hsend.at[i]).wait()
    for k in (0, 4):
        for j in range(1, 4):
            arrived(st.at[k], s_stsend.at[k + j])

    def out_step(b, _):
        outs = (
            (ub.at[b, pl.ds(64, 256)], u_out), (hb.at[b, pl.ds(64, 256)], h_out),
            (tb.at[b], t_out), (nmb.at[b], nm_out), (ntb.at[b], nt_out),
        )
        for i, (src, dst) in enumerate(outs):
            pltpu.make_async_copy(src, dst.at[b], s_out.at[i, b]).wait()
        return 0

    lax.fori_loop(0, REQ, out_step, 0)


def gather_call(*args):
    hbm = pl.BlockSpec(memory_space=pl.ANY)
    vm = pl.BlockSpec(memory_space=pltpu.VMEM)
    sm = pl.BlockSpec(memory_space=pltpu.SMEM)
    dma = pltpu.SemaphoreType.DMA
    return pl.pallas_call(
        gather_kernel,
        out_shape=(
            jax.ShapeDtypeStruct((8, ROWS, 256), BF16),
            jax.ShapeDtypeStruct((REQ, 256, CH), F32),
            jax.ShapeDtypeStruct((REQ, 256, CH), BF16),
            jax.ShapeDtypeStruct((REQ, 256, CH), BF16),
            jax.ShapeDtypeStruct((REQ, 3, 384, 256), BF16),
            jax.ShapeDtypeStruct((REQ, 384, 192), BF16),
        ),
        in_specs=[sm, vm, hbm, vm, hbm, vm, hbm, hbm, hbm, vm, vm, hbm],
        out_specs=(hbm,) * 6,
        scratch_shapes=[
            pltpu.VMEM((ROWS, 256), BF16),
            pltpu.VMEM((8, WHR, CH), BF16),
            pltpu.VMEM((3, 3, CH, CH), BF16),
            pltpu.VMEM((CH, CH), BF16),
            pltpu.VMEM((CH, CH), BF16),
            pltpu.VMEM((48, CH), BF16),
            pltpu.VMEM((REQ, 6, 64, 192), BF16),
            pltpu.VMEM((2, REQ, 4, 256), BF16),
            pltpu.VMEM((REQ, 384, 128), BF16),
            pltpu.VMEM((REQ, 384, CH), BF16),
            pltpu.VMEM((REQ, 384, CH), BF16),
            pltpu.VMEM((REQ, 3, 384, CH), BF16),
            pltpu.VMEM((REQ, 256, CH), F32),
            pltpu.VMEM((REQ, 3, 384, 256), BF16),
            pltpu.VMEM((REQ, 384, 192), BF16),
            pltpu.VMEM((3, 3, CH, CH), BF16),
            pltpu.VMEM((32, CH), F32),
            pltpu.VMEM((8, 32, 128), F32),
            pltpu.VMEM((32, CH), F32),
            dma((12,)), dma((48,)), dma((4,)), dma((4,)), dma, dma, dma, dma,
            dma((4,)), dma((4,)), dma((8,)), dma((8,)), dma((7,)), dma((5, REQ)),
        ],
        compiler_params=pltpu.CompilerParams(
            collective_id=0, has_side_effects=True, vmem_limit_bytes=60 << 20
        ),
        name="gather",
    )(*args)


def control_kernel(ids, scale, valid, wb, nm, nt, hb, ub, tb, o0, o1):
    b = pl.program_id(0)
    w = scale[b] * valid[b].astype(F32)

    def dot(a, k):
        return jnp.dot(a, k, preferred_element_type=F32)

    def proj(h, zm, lane, ktail):
        ha, hc, ht = h[:, 0:128], h[:, 128:256], h[:, 256:320]
        main = dot(h[:, 0:256], wb[0, zm : zm + 256, :]) + dot(ht, wb[0, zm + 256 : zm + 320, :])
        zt = wb[0, O_ZT : O_ZT + 128, :]
        tail = dot(ha, zt[:, lane : lane + 64]) + dot(hc, zt[:, 128 + lane : 192 + lane]) + dot(ht, ktail)
        return jnp.concatenate([main, tail], axis=1).astype(BF16).astype(F32)

    h0 = hb[0]
    r0 = proj(h0, O_Z0, 0, wb[0, O_N + 192 : O_N + 256, 192:256])
    o0[0] = (ub[0].astype(F32) + w * r0).astype(BF16).reshape(4, 64, CH)

    main = jnp.zeros((256, 256), F32)
    side = jnp.zeros((256, 192), F32)
    tail = jnp.zeros((256, 64), F32)
    for i in range(3):
        rows = slice(i * 64, i * 64 + 256)
        for j in range(3):
            k = O_M + (i * 3 + j) * 256
            main = main + dot(nm[0, j, rows, :], wb[0, k : k + 256, :])
        k, n = O_K + i * 192, O_N + i * 256
        main = main + dot(nt[0, rows, :], wb[0, k : k + 192, :])
        side = side + dot(nm[0, 1, rows, :], wb[0, n : n + 256, 0:192])
        tail = tail + dot(nt[0, rows, :], wb[0, n : n + 192, 192:256])
    col = lax.rem(lax.broadcasted_iota(jnp.int32, (256, 64), 0), 64)
    left = jnp.where(col == 0, 0.0, pltpu.roll(side[:, 0:64], 1, 0))
    right = jnp.where(col == 63, 0.0, pltpu.roll(side[:, 128:192], 255, 0))
    tail = tail + left + side[:, 64:128] + right
    h1 = (h0.astype(F32) + jnp.concatenate([main, tail], axis=1)).astype(BF16)
    r1 = proj(h1, O_Z1, 64, wb[0, O_N + 448 : O_N + 512, 192:256])
    o1[0] = (tb[0] + w * r1).astype(BF16).reshape(4, 64, CH)


def control_call(ids, scale, valid, g, nm, nt, hb, ub, tb):
    def mine(shape):
        zeros = (0,) * (len(shape) - 1)
        return pl.BlockSpec(shape, lambda b, *_: (b,) + zeros)

    out = jax.ShapeDtypeStruct((REQ, 4, 64, CH), BF16)
    return pl.pallas_call(
        control_kernel,
        out_shape=(out, out),
        grid_spec=pltpu.PrefetchScalarGridSpec(
            num_scalar_prefetch=3,
            grid=(REQ,),
            in_specs=[
                pl.BlockSpec((1, ROWS, 256), lambda b, ids, *_: (ids[b], 0, 0)),
                mine((1, 3, 384, 256)),
                mine((1, 384, 192)),
                mine((1, 256, CH)),
                mine((1, 256, CH)),
                mine((1, 256, CH)),
            ],
            out_specs=[mine((1, 4, 64, CH)), mine((1, 4, 64, CH))],
        ),
        compiler_params=pltpu.CompilerParams(
            dimension_semantics=("arbitrary",), vmem_limit_bytes=60 << 20
        ),
        name="control",
    )(ids, scale, valid, g, nm, nt, hb, ub, tb)


def shards(
    latent, hint, cond_ids, valid, cond_scale,
    ctl_in, ctl_hint, ctl_zero0, ctl_gain, ctl_conv, ctl_zero1,
    unet_in, unet_gain, unet_conv,
):
    ids = cond_ids[:, 0]
    g, t, u, h, nm, nt = gather_call(
        ids, latent, hint, ctl_in, ctl_hint, ctl_gain, ctl_conv, ctl_zero0, ctl_zero1,
        unet_in, unet_gain, unet_conv,
    )
    return control_call(ids, cond_scale, valid, g, nm, nt, h, u, t)


def solution(mesh):
    n, r = "net", "rep"
    return jax.shard_map(
        shards,
        mesh=mesh,
        in_specs=(
            P(n, r, None), P(n, r, None, None), P(n, None), P(n), P(n),
            P(n, None, None, None, None), P(n, None, None), P(n, None, None), P(n, None),
            P(n, None, None, None, None), P(n, None, None), P(), P(), P(),
        ),
        out_specs=(P(n, r, None, None), P(n, r, None, None)),
        check_vma=False,
    )
```

```python
import functools

import jax
import jax.numpy as jnp
from jax import lax
from jax.experimental import pallas as pl
from jax.experimental.pallas import tpu as pltpu
from jax.sharding import PartitionSpec as P

MESH = pl.DeviceIdType.MESH
F32, BF16 = jnp.float32, jnp.bfloat16
CH = 320
GROUPS = 32
REQ = 8
EPS = 1e-5
O_M, O_K, O_N, O_Z1, O_Z0, O_ZT, ROWS = 0, 2304, 2880, 3648, 3968, 4288, 4416
CHUNK = 256
E2 = 16 * CHUNK
E2N = ROWS - E2
E2H = E2N // 2
WHR = 256


def gray(v):
    return v + lax.div(v, 2) - 2 * lax.div(v, 3)


def gather_kernel(
    ids, lat, hint, cin, chint, cgain, conv, z0, z1, uin, ugain, uconv,
    g, t_out, u_out, h_out, nm_out, nt_out,
    blob, whs, cv, z0v, z1v, wu, hintb, latb, lat48, ub, hb, mb, tb, nmb, ntb, ucv, raw, st, fin,
    s_x, s_yz, s_e, s_wh, s_sib, s_whsib, s_send, s_whsend,
    s_halo, s_hsend, s_st, s_stsend, s_loc, s_out,
):
    net, rep = lax.axis_index("net"), lax.axis_index("rep")
    x, c = lax.div(net, 2), lax.rem(net, 2)
    y, z = lax.div(rep, 4), lax.rem(rep, 4)

    def dev(dx=0, dy=0, dz=0, dc=0):
        return (
            lax.rem(x + dx, 4) * 2 + lax.rem(c + dc, 2),
            lax.rem(y + dy, 4) * 4 + lax.rem(z + dz, 4),
        )

    def rdev(d):
        return (net, lax.rem(rep + d, 16))

    def colour(q, dy=0, dz=0):
        yy, zz = lax.rem(y + dy, 4), lax.rem(z + dz, 4)
        a, b = (yy, zz) if q == 0 else (zz, yy)
        ga, odd = gray(a), lax.rem(b, 2)
        return ga + odd * (3 - 2 * ga)

    def net_of(dx):
        return lax.rem(x + dx, 4) * 2 + c

    barrier = pltpu.get_barrier_semaphore()
    partners = [
        dev(dx=1), dev(dx=3), dev(dc=1), dev(dy=1), dev(dy=3), dev(dy=2),
        dev(dz=1), dev(dz=3), dev(dz=2), rdev(1), rdev(15),
    ]
    for p in partners:
        pl.semaphore_signal(barrier, inc=1, device_id=p, device_id_type=MESH)

    loads = [
        pltpu.make_async_copy(conv.at[0], cv, s_loc.at[0]),
        pltpu.make_async_copy(z0.at[0], z0v, s_loc.at[1]),
        pltpu.make_async_copy(z1.at[0], z1v, s_loc.at[2]),
        pltpu.make_async_copy(chint.at[0], whs.at[net, pl.ds(0, 192)], s_loc.at[3]),
        pltpu.make_async_copy(hint, hintb.at[:, pl.ds(1, 4)], s_loc.at[4]),
        pltpu.make_async_copy(uconv, ucv, s_loc.at[5]),
    ]
    for cp in loads:
        cp.start()

    def input_rows(block):
        parts = [block[i].astype(F32) for i in (2, 1, 0)] + [jnp.zeros((4, CH), F32)]
        return jnp.concatenate(parts, axis=0).astype(BF16)

    for i in range(3):
        whs[net, 192 + 16 * i : 208 + 16 * i, :] = input_rows(cin[0, i])
        wu[16 * i : 16 * i + 16, :] = input_rows(uin[i])
    whs[net, 240:256, :] = jnp.broadcast_to(cgain[...].astype(F32), (16, CH)).astype(BF16)

    loads[3].wait()

    pl.semaphore_wait(barrier, len(partners))

    def send(src, dst, sem, where, ssem):
        pltpu.make_async_remote_copy(
            src_ref=src, dst_ref=dst, send_sem=ssem, recv_sem=sem,
            device_id=where, device_id_type=MESH,
        ).start()

    def arrived(ref, sem):
        pltpu.make_async_copy(ref, ref, sem).wait()

    EV = {}
    for q in range(2):
        for h in range(2):
            EV["L", q, h] = (3, q, h, q * 2 + h)
            EV["R", q, h] = (1, q, h, 4 + q * 2 + h)
        EV["LL", q] = (2, q, 0, 8 + q)
        EV["RR", q] = (2, q, 1, 10 + q)

    def rows_of(q, h, dy=0, dz=0):
        start = pl.multiple_of((colour(q, dy, dz) * 2 + (q * 8 + h)) * CHUNK, CHUNK)
        return pl.ds(start, CHUNK)

    def own_chunk(q, h):
        r = rows_of(q, h)
        send(blob.at[r], g.at[net, r], s_x.at[EV["L", q, h][3]], dev(dx=1), s_send)
        send(blob.at[r], g.at[net, r], s_x.at[EV["R", q, h][3]], dev(dx=3), s_send)

    def x_relay(key):
        dx, q, h, _ = EV[key]
        ref = g.at[net_of(dx), rows_of(q, h)]
        if key[0] == "L":
            send(ref, ref, s_x.at[EV["LL", q][3]], dev(dx=1), s_send)
        else:
            send(ref, ref, s_x.at[EV["RR", q][3]], dev(dx=3), s_send)

    def to_sib(ref):
        send(ref, ref, s_sib, dev(dc=1), s_send)

    def dirs(q, h):
        main, other = ((0, 1), (2, 3)) if q == 0 else ((2, 3), (0, 1))
        return main + (other[h],)

    STEP = [dict(dy=1), dict(dy=3), dict(dz=1), dict(dz=3)]
    BACK = [dict(dy=3), dict(dy=1), dict(dz=3), dict(dz=1)]

    def x_event(key):
        dx, q, h, sem = EV[key]
        ref = g.at[net_of(dx), rows_of(q, h)]
        arrived(ref, s_x.at[sem])
        for d in dirs(q, h):
            send(ref, ref, s_yz.at[d * 12 + sem], dev(**STEP[d]), s_send)
        to_sib(ref)

    def yz_event(key):
        dx, q, h, sem = EV[key]
        for d in dirs(q, h):
            ref = g.at[net_of(dx), rows_of(q, h, **BACK[d])]
            arrived(ref, s_yz.at[d * 12 + sem])
            to_sib(ref)

    e2r, e2h = pl.ds(E2, E2N), (pl.ds(E2, E2H), pl.ds(E2 + E2H, E2H))

    def own_e2():
        send(blob.at[e2r], g.at[net, e2r], s_e.at[0], dev(dx=1), s_send)
        send(blob.at[e2r], g.at[net, e2r], s_e.at[1], dev(dx=3), s_send)

    def e2_event():
        for i, dx, to in ((0, 3, 1), (1, 1, 3)):
            ref = g.at[net_of(dx), e2r]
            arrived(ref, s_e.at[i])
            half = g.at[net_of(dx), e2h[i]]
            send(half, half, s_e.at[2 + i], dev(dx=to), s_send)
            to_sib(ref)

    def e2_far():
        for i in range(2):
            ref = g.at[net_of(2), e2h[i]]
            arrived(ref, s_e.at[2 + i])
            to_sib(ref)

    whh = (pl.ds(0, WHR // 2), pl.ds(WHR // 2, WHR // 2))

    def wh_sib(ref):
        send(ref, ref, s_whsib, dev(dc=1), s_whsend)

    def wh_event():
        for i, dx, to in ((0, 3, 1), (1, 1, 3)):
            ref = whs.at[net_of(dx)]
            arrived(ref, s_wh.at[i])
            half = whs.at[net_of(dx), whh[i]]
            send(half, half, s_wh.at[2 + i], dev(dx=to), s_whsend)
            wh_sib(ref)

    def wh_far():
        for i in range(2):
            ref = whs.at[net_of(2), whh[i]]
            arrived(ref, s_wh.at[2 + i])
            wh_sib(ref)
        arrived(whs.at[pl.ds(0, 4)], s_whsib)

    halos = [
        (lat, latb.at[0], rdev(1)), (lat, latb.at[1], rdev(15)),
        (hint.at[:, 3], hintb.at[:, 0], rdev(1)), (hint.at[:, 0], hintb.at[:, 5], rdev(15)),
    ]
    for i, (src, dst, to) in enumerate(halos[:2]):
        send(src, dst, s_halo.at[i], to, s_hsend.at[i])
    mine = whs.at[net]
    send(mine, mine, s_wh.at[0], dev(dx=1), s_whsend)
    send(mine, mine, s_wh.at[1], dev(dx=3), s_whsend)
    send(mine, mine, s_whsib, dev(dc=1), s_whsend)
    for i, (src, dst, to) in enumerate(halos):
        if i >= 2:
            send(src, dst, s_halo.at[i], to, s_hsend.at[i])

    for cp in loads[:3]:
        cp.wait()
    for i in range(3):
        for j in range(3):
            k = i * 3 + j
            blob[O_M + k * 256 : O_M + k * 256 + 256, :] = cv[i, j, 0:256, 0:256]
            blob[O_K + k * 64 : O_K + k * 64 + 64, :] = cv[i, j, 256:CH, 0:256]
        n = O_N + i * 256
        if i < 2:
            zk = (z0v, z1v)[i][256:CH, 256:CH]
        else:
            zk = jnp.zeros((64, 64), BF16)
        kt = jnp.concatenate([cv[i, j, 256:CH, 256:CH] for j in range(3)] + [zk], axis=0)
        nt = [cv[i, j, 0:256, 256:CH] for j in range(3)]
        blob[n : n + 256, :] = jnp.concatenate(nt + [kt], axis=1)
    blob[O_Z1 : O_Z1 + CH, :] = z1v[:, 0:256]
    blob[O_Z0 : O_Z0 + CH, :] = z0v[:, 0:256]
    zt = [zv[k : k + 128, 256:CH] for k in (0, 128) for zv in (z0v, z1v)]
    blob[O_ZT : O_ZT + 128, :] = jnp.concatenate(zt, axis=1)
    own_blob = pltpu.make_async_copy(blob, g.at[net], s_loc.at[6])
    own_blob.start()

    def run(todo):
        for name, key in todo:
            if name == "x":
                x_event(key)
            elif name == "yz":
                yz_event(key)
            elif name == "relay":
                x_relay(key)
            elif name == "own":
                own_chunk(*key)
            else:
                key()

    def loop(first, last, piece, after):
        def body(b, _):
            piece(b)
            for k, todo in after.items():
                @pl.when(b == k)
                def _():
                    run(todo)
            return 0

        lax.fori_loop(first, last, body, 0)

    for i in range(2):
        arrived(latb.at[i], s_halo.at[i])
    li = lax.broadcasted_iota(jnp.int32, (256, 256), 0)
    lj = lax.broadcasted_iota(jnp.int32, (256, 256), 1)
    perm = (lj == (252 - (li - lax.rem(li, 4)) + lax.rem(li, 4))).astype(BF16)
    xs = lax.broadcasted_iota(jnp.int32, (64, 128), 0)
    ls = lax.broadcasted_iota(jnp.int32, (64, 128), 1)
    keep = (ls < 12) & ~((ls < 4) & (xs == 63)) & ~((ls >= 8) & (xs == 0))

    def lat_step(b):
        rolled = []
        above = jnp.where(rep > 0, latb[0, b].astype(F32)[2:4], 0.0)
        below = jnp.where(rep < 15, latb[1, b].astype(F32)[0:2], 0.0)
        rows = jnp.concatenate([above, lat[b].astype(F32), below], axis=0).astype(BF16)
        rows = jnp.dot(rows, perm, preferred_element_type=F32)
        for r in range(8):
            row = rows[r : r + 1]
            skew = pltpu.roll(jnp.broadcast_to(row, (8, 256)), 0, 1, stride=4, stride_axis=0)
            full = [pltpu.roll(skew, 8 + 32 * k, 1)[:, :128] for k in range(8)]
            rolled.append(jnp.where(keep, jnp.concatenate(full, axis=0), 0.0))
        for r in range(6):
            v = rolled[r] + pltpu.roll(rolled[r + 1], 16, 1) + pltpu.roll(rolled[r + 2], 32, 1)
            lat48[b, pl.ds(r * 64, 64), :] = v.astype(BF16)

    loop(0, REQ, lat_step, {
        5: [("wh", wh_event)] + [("own", (q, h)) for h in range(2) for q in range(2)],
    })

    def sums(row, v):
        f = v[64:320].astype(F32)
        raw[pl.ds(row, 1), :] = jnp.sum(f, axis=0, keepdims=True)
        raw[pl.ds(8 + row, 1), :] = jnp.sum(f * f, axis=0, keepdims=True)

    def u_step(b, _):
        v = jnp.dot(lat48[b, :, 0:48], wu[...], preferred_element_type=F32).astype(BF16)
        ub[b] = v
        sums(b, v)
        pltpu.make_async_copy(ub.at[b, pl.ds(64, 256)], u_out.at[b], s_out.at[0, b]).start()
        return 0

    lax.fori_loop(0, REQ, u_step, 0)

    wh_far()
    send(blob, g.at[net], s_sib, dev(dc=1), s_send)
    loads[4].wait()
    for i in range(2, 4):
        arrived(hintb.at[:, 0], s_halo.at[i])

    def h_step(b):
        n = ids[b]
        w = whs[n]
        v = jnp.dot(hintb[b].reshape(384, 192), w[0:192], preferred_element_type=F32)
        v = v + jnp.dot(lat48[b, :, 0:48], w[192:240], preferred_element_type=F32)
        v = v.astype(BF16)
        hb[b] = v
        sums(16 + b, v)
        pltpu.make_async_copy(hb.at[b, pl.ds(64, 256)], h_out.at[b], s_out.at[1, b]).start()

    loop(0, REQ, h_step, {})

    def stats_send(k, axis):
        for j in range(1, 4):
            send(st.at[k], st.at[k + j], s_st.at[k + j], dev(**{axis: j}), s_stsend.at[k + j])

    def stats_sum(k):
        total = st[k]
        for j in range(1, 4):
            arrived(st.at[k + j], s_st.at[k + j])
            total = total + st[k + j]
        return total

    gsz = CH // GROUPS
    gi = lax.broadcasted_iota(jnp.int32, (CH, 128), 0)
    gj = lax.broadcasted_iota(jnp.int32, (CH, 128), 1)
    member = (lax.div(gi, gsz) == gj).astype(F32)
    st[0] = jnp.dot(raw[...], member, preferred_element_type=F32, precision=lax.Precision.HIGHEST)
    stats_send(0, "dz")
    st[4] = stats_sum(0)
    stats_send(4, "dy")
    run([("x", ("L", 0, 0)), ("x", ("R", 0, 0)), ("x", ("L", 1, 0)), ("x", ("R", 1, 0))])
    run([("relay", ("L", 0, 0)), ("relay", ("L", 1, 0))])

    per = stats_sum(4) * (1.0 / (64 * 64 * gsz))
    for k in (0, 16):
        m, q = per[k : k + 8], per[k + 8 : k + 16]
        both = jnp.concatenate([m, lax.rsqrt(q - m * m + EPS)], axis=0)
        fin[k : k + 16, :] = lax.dot_general(
            both, member, (((1,), (1,)), ((), ())),
            preferred_element_type=F32, precision=lax.Precision.HIGHEST,
        )

    pos = lax.broadcasted_iota(jnp.int32, (384, CH), 0)
    col = lax.rem(pos, 64)
    inside = ((pos >= 64) | (rep > 0)) & ((pos < 320) | (rep < 15))

    def normed(v, row, gain):
        m = fin[pl.ds(row, 1), :]
        s = fin[pl.ds(8 + row, 1), :] * gain
        n = (v.astype(F32) - m) * s
        n = n / (1.0 + jnp.exp(-n))
        n = jnp.where(inside, n, 0.0)
        left = jnp.where(col == 0, 0.0, pltpu.roll(n, 1, 0))
        right = jnp.where(col == 63, 0.0, pltpu.roll(n, 383, 0))
        return left, n, right

    def m_step(b):
        for i, v in enumerate(normed(ub[b], b, ugain[...].astype(F32).reshape(1, CH))):
            mb[b, i] = v.astype(BF16)

    loop(0, REQ, m_step, {
        1: [("x", ("L", 0, 1)), ("x", ("R", 0, 1)), ("relay", ("R", 0, 1))],
        3: [("yz", ("L", 0, 0))],
        5: [("x", ("L", 1, 1)), ("x", ("R", 1, 1)), ("relay", ("R", 1, 1)), ("e2", own_e2)],
        7: [("yz", ("R", 0, 0))],
    })

    loads[5].wait()

    def conv_step(b):
        acc = ub[b, 64:320, :].astype(F32)
        for i in range(3):
            for j in range(3):
                acc = acc + jnp.dot(
                    mb[b, j, pl.ds(i * 64, 256), :], ucv[i, j], preferred_element_type=F32
                )
        tb[b] = acc
        pltpu.make_async_copy(tb.at[b], t_out.at[b], s_out.at[2, b]).start()

    loop(0, REQ, conv_step, {
        0: [("yz", ("L", 1, 0))],
        1: [("x", ("LL", 0)), ("x", ("RR", 0))],
        2: [("x", ("LL", 1)), ("x", ("RR", 1))],
        3: [("yz", ("R", 1, 0))],
        5: [("yz", ("L", 0, 1)), ("yz", ("L", 1, 1))],
        7: [("yz", ("R", 0, 1)), ("yz", ("R", 1, 1))],
    })

    def n_step(b):
        n = ids[b]
        gain = whs[n, 240:256, :][0:1].astype(F32)
        parts = [v.astype(BF16) for v in normed(hb[b], 16 + b, gain)]
        for i, v in enumerate(parts):
            nmb[b, i] = v[:, 0:256]
        ntb[b] = jnp.concatenate([v[:, 256:320] for v in parts], axis=1)
        pltpu.make_async_copy(nmb.at[b], nm_out.at[b], s_out.at[3, b]).start()
        pltpu.make_async_copy(ntb.at[b], nt_out.at[b], s_out.at[4, b]).start()

    loop(0, REQ, n_step, {7: [("yz", ("LL", 0))]})
    e2_event()
    run([("yz", ("RR", 0)), ("yz", ("LL", 1)), ("yz", ("RR", 1))])
    e2_far()

    arrived(g.at[pl.ds(0, 4)], s_sib)
    arrived(g.at[pl.ds(0, 7)], s_send)
    arrived(whs.at[pl.ds(0, 7)], s_whsend)
    own_blob.wait()
    for i in range(4):
        src = halos[i][0]
        pltpu.make_async_copy(src, src, s_hsend.at[i]).wait()
    for k in (0, 4):
        for j in range(1, 4):
            arrived(st.at[k], s_stsend.at[k + j])

    def out_step(b, _):
        outs = (
            (ub.at[b, pl.ds(64, 256)], u_out), (hb.at[b, pl.ds(64, 256)], h_out),
            (tb.at[b], t_out), (nmb.at[b], nm_out), (ntb.at[b], nt_out),
        )
        for i, (src, dst) in enumerate(outs):
            pltpu.make_async_copy(src, dst.at[b], s_out.at[i, b]).wait()
        return 0

    lax.fori_loop(0, REQ, out_step, 0)


def gather_call(*args):
    hbm = pl.BlockSpec(memory_space=pl.ANY)
    vm = pl.BlockSpec(memory_space=pltpu.VMEM)
    sm = pl.BlockSpec(memory_space=pltpu.SMEM)
    dma = pltpu.SemaphoreType.DMA
    return pl.pallas_call(
        gather_kernel,
        out_shape=(
            jax.ShapeDtypeStruct((8, ROWS, 256), BF16),
            jax.ShapeDtypeStruct((REQ, 256, CH), F32),
            jax.ShapeDtypeStruct((REQ, 256, CH), BF16),
            jax.ShapeDtypeStruct((REQ, 256, CH), BF16),
            jax.ShapeDtypeStruct((REQ, 3, 384, 256), BF16),
            jax.ShapeDtypeStruct((REQ, 384, 192), BF16),
        ),
        in_specs=[sm, vm, hbm, vm, hbm, vm, hbm, hbm, hbm, vm, vm, hbm],
        out_specs=(hbm,) * 6,
        scratch_shapes=[
            pltpu.VMEM((ROWS, 256), BF16),
            pltpu.VMEM((8, WHR, CH), BF16),
            pltpu.VMEM((3, 3, CH, CH), BF16),
            pltpu.VMEM((CH, CH), BF16),
            pltpu.VMEM((CH, CH), BF16),
            pltpu.VMEM((48, CH), BF16),
            pltpu.VMEM((REQ, 6, 64, 192), BF16),
            pltpu.VMEM((2, REQ, 4, 256), BF16),
            pltpu.VMEM((REQ, 384, 128), BF16),
            pltpu.VMEM((REQ, 384, CH), BF16),
            pltpu.VMEM((REQ, 384, CH), BF16),
            pltpu.VMEM((REQ, 3, 384, CH), BF16),
            pltpu.VMEM((REQ, 256, CH), F32),
            pltpu.VMEM((REQ, 3, 384, 256), BF16),
            pltpu.VMEM((REQ, 384, 192), BF16),
            pltpu.VMEM((3, 3, CH, CH), BF16),
            pltpu.VMEM((32, CH), F32),
            pltpu.VMEM((8, 32, 128), F32),
            pltpu.VMEM((32, CH), F32),
            dma((12,)), dma((48,)), dma((4,)), dma((4,)), dma, dma, dma, dma,
            dma((4,)), dma((4,)), dma((8,)), dma((8,)), dma((7,)), dma((5, REQ)),
        ],
        compiler_params=pltpu.CompilerParams(
            collective_id=0, has_side_effects=True, vmem_limit_bytes=60 << 20
        ),
        name="gather",
    )(*args)


def control_kernel(ids, scale, valid, wb, nm, nt, hb, ub, tb, o0, o1):
    b = pl.program_id(0)
    w = scale[b] * valid[b].astype(F32)

    def dot(a, k):
        return jnp.dot(a, k, preferred_element_type=F32)

    def proj(h, zm, lane, ktail):
        ha, hc, ht = h[:, 0:128], h[:, 128:256], h[:, 256:320]
        main = dot(h[:, 0:256], wb[0, zm : zm + 256, :]) + dot(ht, wb[0, zm + 256 : zm + 320, :])
        zt = wb[0, O_ZT : O_ZT + 128, :]
        tail = dot(ha, zt[:, lane : lane + 64]) + dot(hc, zt[:, 128 + lane : 192 + lane]) + dot(ht, ktail)
        return jnp.concatenate([main, tail], axis=1).astype(BF16).astype(F32)

    h0 = hb[0]
    r0 = proj(h0, O_Z0, 0, wb[0, O_N + 192 : O_N + 256, 192:256])
    o0[0] = (ub[0].astype(F32) + w * r0).astype(BF16).reshape(4, 64, CH)

    rows = [slice(i * 64, i * 64 + 256) for i in range(3)]
    lhs = jnp.concatenate([nm[0, j, r, :] for r in rows for j in range(3)], axis=1)
    main = dot(lhs, wb[0, O_M:O_K, :])
    lhs = jnp.concatenate([nm[0, 1, r, :] for r in rows], axis=1)
    side = dot(lhs, wb[0, O_N:O_Z1, 0:192])
    tail = jnp.zeros((256, 64), F32)
    for i in range(3):
        k, n = O_K + i * 192, O_N + i * 256
        part = nt[0, rows[i], :]
        main = main + dot(part, wb[0, k : k + 192, :])
        tail = tail + dot(part, wb[0, n : n + 192, 192:256])
    col = lax.rem(lax.broadcasted_iota(jnp.int32, (256, 64), 0), 64)
    left = jnp.where(col == 0, 0.0, pltpu.roll(side[:, 0:64], 1, 0))
    right = jnp.where(col == 63, 0.0, pltpu.roll(side[:, 128:192], 255, 0))
    tail = tail + left + side[:, 64:128] + right
    h1 = (h0.astype(F32) + jnp.concatenate([main, tail], axis=1)).astype(BF16)
    r1 = proj(h1, O_Z1, 64, wb[0, O_N + 448 : O_N + 512, 192:256])
    o1[0] = (tb[0] + w * r1).astype(BF16).reshape(4, 64, CH)


def control_call(ids, scale, valid, g, nm, nt, hb, ub, tb):
    def mine(shape):
        zeros = (0,) * (len(shape) - 1)
        return pl.BlockSpec(shape, lambda b, *_: (b,) + zeros)

    out = jax.ShapeDtypeStruct((REQ, 4, 64, CH), BF16)
    return pl.pallas_call(
        control_kernel,
        out_shape=(out, out),
        grid_spec=pltpu.PrefetchScalarGridSpec(
            num_scalar_prefetch=3,
            grid=(REQ,),
            in_specs=[
                pl.BlockSpec((1, ROWS, 256), lambda b, ids, *_: (ids[b], 0, 0)),
                mine((1, 3, 384, 256)),
                mine((1, 384, 192)),
                mine((1, 256, CH)),
                mine((1, 256, CH)),
                mine((1, 256, CH)),
            ],
            out_specs=[mine((1, 4, 64, CH)), mine((1, 4, 64, CH))],
        ),
        compiler_params=pltpu.CompilerParams(
            dimension_semantics=("arbitrary",), vmem_limit_bytes=60 << 20
        ),
        name="control",
    )(ids, scale, valid, g, nm, nt, hb, ub, tb)


def shards(
    latent, hint, cond_ids, valid, cond_scale,
    ctl_in, ctl_hint, ctl_zero0, ctl_gain, ctl_conv, ctl_zero1,
    unet_in, unet_gain, unet_conv,
):
    ids = cond_ids[:, 0]
    g, t, u, h, nm, nt = gather_call(
        ids, latent, hint, ctl_in, ctl_hint, ctl_gain, ctl_conv, ctl_zero0, ctl_zero1,
        unet_in, unet_gain, unet_conv,
    )
    return control_call(ids, cond_scale, valid, g, nm, nt, h, u, t)


def solution(mesh):
    n, r = "net", "rep"
    return jax.shard_map(
        shards,
        mesh=mesh,
        in_specs=(
            P(n, r, None), P(n, r, None, None), P(n, None), P(n), P(n),
            P(n, None, None, None, None), P(n, None, None), P(n, None, None), P(n, None),
            P(n, None, None, None, None), P(n, None, None), P(), P(), P(),
        ),
        out_specs=(P(n, r, None, None), P(n, r, None, None)),
        check_vma=False,
    )
```
